128 devices in a mesh: seq: 8 (over y, core), tile: 16 (over z, x).
Axes of the slice: x: 4, y: 4, z: 4, core: 2. Of those that a mesh axis runs over, the one named last changes fastest.
Arguments:
- latents: bfloat16 [16384, 128], P(('seq', 'tile')), may hold values from -6 to 6
- grid_slot: int32 [16384], P(('seq', 'tile')), may hold values from 0 to 16383, as said below
- w_in: bfloat16 [432, 384], replicated, may hold values from -0.3125 to 0.3125
- b_in: float32 [384], replicated, may hold values from -3 to 3
- gain_in: float32 [384], replicated, may hold values from 0.1 to 1.9
- w_up: bfloat16 [3456, 192], replicated, may hold values from -0.109375 to 0.109375
- b_up: float32 [192], replicated, may hold values from -3 to 3
- gain_res: float32 [192], replicated, may hold values from 0.1 to 1.9
- w_res: bfloat16 [5184, 192], replicated, may hold values from -0.078125 to 0.078125
- b_res: float32 [192], replicated, may hold values from -3 to 3
Outputs:
- decoded: bfloat16 [16, 128, 49152], P(None, 'tile', 'seq')
The draws below stay inside these ranges and needn't reach their ends.
Inputs may be any that keep to these rules, and one draw needn't show every extreme that they name: grid_slot is a permutation of 0 to 16383. Row r of the sequence lies on device r // 128 and grid row p on device p // 128 (devices in the order seq then tile). The rows of one device go to exactly 64 receiving devices, exactly 2 rows to each, so every device receives 128 rows; the receivers of device d are d + k modulo 128 for a set of offsets k common to all devices, which includes 128 / 2.
All inputs are finite; a program needn't handle non-finite values.
Results may differ from the reference program's by a relative error of at most 0.0058.
Values may be sent and summed in bfloat16 or wider, within the bound.
No kernel may reach another device: no remote copies, remote signals or barrier semaphores. Data moves between devices by JAX's collectives and lax.ppermute only.
A program may use at most 192 MiB of HBM per device.

```python
import jax
import jax.numpy as jnp
from jax import lax

LAT = 16
C1 = 384
C2 = 192
FS = 2
TH = 4
W = 128
F = 16
H = 64
ROW_DEV = 128
ROWS = 16384
CAP = 2
N_SEQ = 8
N_TILE = 16
DEVICES = 128


def draw_grid_slot(key, part):
    groups = ROW_DEV // CAP
    half = DEVICES // 2
    first_key, second_key, third_key = jax.random.split(key, 3)
    source_order = jax.vmap(lambda subkey: jax.random.permutation(subkey, ROW_DEV))(jax.random.split(first_key, DEVICES)).astype(jnp.int32)
    others = jax.random.permutation(second_key, DEVICES - 1).astype(jnp.int32)
    others = others + (others >= half).astype(jnp.int32)
    offsets = jnp.concatenate([jnp.full((1,), half, jnp.int32), others[:groups - 1]]).astype(jnp.int32)
    arrival_order = jax.vmap(lambda subkey: jax.random.permutation(subkey, ROW_DEV))(jax.random.split(third_key, DEVICES)).astype(jnp.int32)
    group_of = source_order // CAP
    source = jnp.arange(DEVICES, dtype=jnp.int32)[:, None]
    target = (source + offsets[group_of]) % DEVICES
    slot = target * ROW_DEV + arrival_order[target, source_order]
    return slot.reshape(-1).astype(jnp.int32)


def block_levels(key, extent, cuts, smallest, largest):
    level = 1.0
    for axis_at, parts in cuts:
        heights = jax.random.uniform(jax.random.fold_in(jax.random.fold_in(key, 6), axis_at), (parts,), jnp.float32, smallest / len(cuts), largest / len(cuts))
        level = level * jnp.repeat(jnp.exp(heights), extent[axis_at] // parts).reshape((-1,) + (1,) * (len(extent) - 1 - axis_at))
    return level


def gaussian(key, shape, scale, most, shards=(), kind=jnp.bfloat16):
    loudness = block_levels(key, shape, shards, -0.22, 0.18) if shards else 1.0
    entries = jax.random.normal(key, shape, jnp.float32) * scale * loudness
    return jnp.minimum(jnp.maximum(entries, -most), most).astype(kind)


def setup_inputs(seed: int = 0) -> dict:
    key_list = jax.random.split(jax.random.key(seed), 11)
    return {
        "latents": gaussian(key_list[0], (ROWS, 8 * LAT), 1.0, 6.0, ((0, 128),)),
        "grid_slot": draw_grid_slot(jax.random.fold_in(key_list[10], 71), 0),
        "w_in": gaussian(key_list[2], (27 * LAT, C1), (27 * LAT) ** -0.5, 0.3125),
        "b_in": gaussian(key_list[3], (C1,), 0.5, 3.0, (), jnp.float32),
        "gain_in": jnp.clip(1.0 + 0.18 * jax.random.normal(key_list[4], (C1,), jnp.float32), 0.1, 1.9),
        "w_up": gaussian(key_list[5], (9 * C1, C2), (9 * C1) ** -0.5, 0.109375),
        "b_up": gaussian(key_list[6], (C2,), 0.5, 3.0, (), jnp.float32),
        "gain_res": jnp.clip(1.0 + 0.18 * jax.random.normal(key_list[7], (C2,), jnp.float32), 0.1, 1.9),
        "w_res": gaussian(key_list[8], (27 * C2, C2), (27 * C2) ** -0.5, 0.078125),
        "b_res": gaussian(key_list[9], (C2,), 0.5, 3.0, (), jnp.float32),
    }


def causal_taps(padded, weight, bias):
    frames = padded.shape[0] - 2
    height = padded.shape[1] - 2
    breadth = padded.shape[2] - 2
    channels = padded.shape[3]
    running = jnp.zeros((frames * height * breadth, weight.shape[1]), jnp.float32)
    for time_off in range(3):
        for row_off in range(3):
            window = jnp.concatenate([padded[time_off:time_off + frames, row_off:row_off + height, col_off:col_off + breadth] for col_off in range(3)], axis=-1)
            start = (time_off * 3 + row_off) * 3 * channels
            running = running + jnp.dot(window.reshape(-1, 3 * channels), weight[start:start + 3 * channels], preferred_element_type=jnp.float32)
    return (running + bias).reshape(frames, height, breadth, weight.shape[1])

def upsample_conv(extended, weight, bias):
    doubled = jnp.repeat(jnp.repeat(extended, 2, axis=1), 2, axis=2)[:, 1:-1, 1:-1]
    frames = doubled.shape[0]
    height = doubled.shape[1] - 2
    breadth = doubled.shape[2] - 2
    channels = doubled.shape[3]
    running = jnp.zeros((frames * height * breadth, weight.shape[1]), jnp.float32)
    for row_off in range(3):
        window = jnp.concatenate([doubled[:, row_off:row_off + height, col_off:col_off + breadth] for col_off in range(3)], axis=-1)
        start = row_off * 3 * channels
        running = running + jnp.dot(window.reshape(-1, 3 * channels), weight[start:start + 3 * channels], preferred_element_type=jnp.float32)
    return (running + bias).astype(jnp.bfloat16).reshape(frames, height, breadth, weight.shape[1])

def normed_silu(values, gain):
    scaled = values * lax.rsqrt(lax.optimization_barrier(jnp.mean(values * values, axis=-1, keepdims=True)) + 1e-06) * gain
    return jax.nn.silu(scaled).astype(jnp.bfloat16)

def causal_conv(field, weight, bias):
    padded = jnp.pad(field, ((2, 0), (1, 1), (1, 1), (0, 0)))

    def one_frame(index):
        block = lax.dynamic_slice_in_dim(padded, index, 3, 0)
        return causal_taps(block, weight, bias)[0]
    return lax.map(one_frame, jnp.arange(field.shape[0], dtype=jnp.int32))

def reference(latents, grid_slot, w_in, b_in, gain_in, w_up, b_up, gain_res, w_res, b_res):
    grid_rows = jnp.zeros(latents.shape, jnp.bfloat16).at[grid_slot].set(latents)
    grid_latent = grid_rows.reshape(N_SEQ, N_TILE, FS, TH, W, LAT).transpose(0, 2, 1, 3, 4, 5).reshape(F, H, W, LAT)
    first_conv = causal_conv(grid_latent, w_in, b_in)
    first_act = normed_silu(first_conv, gain_in)
    padded_act = jnp.pad(first_act, ((0, 0), (1, 1), (1, 1), (0, 0)))

    def up_frame(frame_act):
        return upsample_conv(frame_act[None], w_up, b_up)[0]
    upsampled = lax.map(up_frame, padded_act)
    res_act = normed_silu(upsampled.astype(jnp.float32), gain_res)
    res_conv = causal_conv(res_act, w_res, b_res)
    decoded = (upsampled.astype(jnp.float32) + res_conv).astype(jnp.bfloat16)
    return decoded.reshape(F, 2 * H, 2 * W * C2)
```

```python
import jax
import jax.numpy as jnp
from jax import lax
from jax.experimental import pallas as pl
from jax.experimental.pallas import tpu as pltpu
from jax.sharding import PartitionSpec as P

F32 = jnp.float32
BF16 = jnp.bfloat16
I32 = jnp.int32


def iota(shape, dim):
    return lax.broadcasted_iota(I32, shape, dim)


def ones_where(cond):
    return jnp.where(cond, 1.0, 0.0).astype(BF16)


def outbox_kernel(slot_ref, lat_ref, out_ref):
    n = 128
    row = jnp.broadcast_to(slot_ref[...], (n, n))
    col = jnp.transpose(row)
    i, j = iota((n, n), 0), iota((n, n), 1)
    same = (row >> 7) == (col >> 7)
    rank_row = jnp.sum(jnp.where(same & (i < j), 1, 0), axis=0, keepdims=True)
    rank_col = jnp.sum(jnp.where(same & (j < i), 1, 0), axis=1, keepdims=True)

    def keys(slot, rank):
        target = slot >> 7
        band = target & 15
        frame, high, group = (slot >> 6) & 1, (slot >> 4) & 3, slot & 15
        upper = high < 2
        halo_target = jnp.where(upper, target - 1, target + 1)
        inside = (upper & (band > 0)) | ((high >= 2) & (band < 15))
        halo_target = jnp.where(inside, halo_target, -1000)
        halo_slot = jnp.where(upper, 4, 2) + rank
        own_label = (frame * 8 + high + 2) * 16 + group + 1
        halo_label = (frame * 8 + jnp.where(upper, high + 6, high - 2)) * 16 + group + 1
        return target, halo_target, halo_slot, own_label, halo_label

    target, halo_target, halo_slot, _, _ = keys(slot_ref[...], rank_row)
    _, _, halo_slot_col, own_label, halo_label = keys(col, rank_col)
    own_table = jnp.where(j == rank_col, own_label, 0).astype(F32).astype(BF16)
    halo_table = jnp.where(j == halo_slot_col, halo_label, 0).astype(F32).astype(BF16)

    q = iota((8 * n, n), 0)
    pick = ones_where((q == target * 8 + rank_row) | (q == halo_target * 8 + halo_slot))
    pick_own = ones_where(q == target * 8 + 6)
    pick_halo = ones_where(q == halo_target * 8 + 6)
    out = jnp.dot(pick, lat_ref[...], preferred_element_type=F32)
    out += jnp.dot(pick_own, own_table, preferred_element_type=F32)
    out += jnp.dot(pick_halo, halo_table, preferred_element_type=F32)
    out_ref[...] = out.astype(BF16)


def route_kernel(inbox_ref, out_ref):
    rows = inbox_ref.shape[0]
    inbox = inbox_ref[...]
    boxes = inbox.astype(F32).reshape(rows // 8, 8, 128)
    labels = jnp.broadcast_to(boxes[:, 6:7, :], boxes.shape)
    slot, lane = iota(boxes.shape, 1), iota(boxes.shape, 2)
    label = jnp.sum(jnp.where((slot == lane) & (slot < 6), labels, 0.0), axis=2, keepdims=True)
    label = label.reshape(rows, 1).astype(I32)
    k = iota((1, 512), 1)
    group = 2 * (k >> 6) - 1 + ((k >> 1) & 3)
    wanted = ((k & 1) * 8 + ((k >> 3) & 7)) * 16 + group + 1
    wanted = jnp.where((group >= 0) & (group < 16), wanted, -1)
    pick = ones_where(label == wanted)
    out = lax.dot_general(pick, inbox, (((0,), (0,)), ((), ())), preferred_element_type=F32)
    out_ref[...] = out.astype(BF16)


def silu(v):
    half = 0.5 * v
    return half * jnp.tanh(half) + half


def decode_kernel(
    recv_ref, w1_ref, b1_ref, g1_ref, wc_ref, bc_ref, g2_ref, w0_ref, wp_ref, b3_ref,
    out_ref, grid_ref, x_ref, a_ref, u_ref, acc_ref, r_ref, fin_ref,
):
    s = lax.axis_index("seq")
    t = lax.axis_index("tile")
    lane = iota((1, 128), 1)

    i, k = iota((1536, 512), 0), iota((1536, 512), 1)
    key_i = ((i >> 4) & 31) * 32 + (i & 15) - 2 + (i >> 9)
    key_k = ((k >> 1) & 31) * 32 + 2 * (k >> 6) + (k & 1)
    grid_ref[...] = jnp.dot(
        ones_where(key_i == key_k), recv_ref[...], preferred_element_type=F32
    ).reshape(3, 8, 4, 16, 128)

    def windows(y, carry):
        tiles = [[grid_ref[d, y, c] for c in range(4)] for d in range(3)]
        for ix in range(18):
            c, o = divmod((ix + 6) * 16, 128)

            def window(d, to):
                tile = tiles[d][c]
                if o + 48 > 128:
                    tile = jnp.where(lane >= o, tile, tiles[d][c + 1])
                shift = (to - o) % 128
                return pltpu.roll(tile, shift, 1) if shift else tile

            x_ref[y, ix, :, 0:128] = jnp.where(lane < 64, window(0, 0), window(1, 64)).astype(BF16)
            x_ref[y, ix, :, 128:256] = window(2, 0).astype(BF16)
        return carry

    lax.fori_loop(0, 8, windows, 0)

    def first(iy, carry):
        lhs = jnp.concatenate([x_ref[iy + d].reshape(288, 256) for d in range(3)], axis=1)
        v = jnp.dot(lhs, w1_ref[...], preferred_element_type=F32) + b1_ref[...]
        scale = lax.rsqrt(jnp.mean(v * v, axis=1, keepdims=True) + 1e-06)
        a_ref[iy] = silu(v * scale * g1_ref[...]).astype(BF16).reshape(18, 16, 384)
        return carry

    lax.fori_loop(0, 6, first, 0)

    @pl.when(t == 0)
    def _():
        a_ref[0] = jnp.zeros((18, 16, 384), BF16)

    @pl.when(t == lax.axis_size("tile") - 1)
    def _():
        a_ref[5] = jnp.zeros((18, 16, 384), BF16)

    @pl.when(s == 0)
    def _():
        a_ref[:, 0] = jnp.zeros((6, 16, 384), BF16)

    @pl.when(s == lax.axis_size("seq") - 1)
    def _():
        a_ref[:, 17] = jnp.zeros((6, 16, 384), BF16)

    def corners(ci, carry):
        lhs = jnp.concatenate(
            [a_ref[ci + d, pl.ds(e, 17)].reshape(272, 384) for d in range(2) for e in range(2)],
            axis=1,
        )
        acc_ref[...] = jnp.dot(lhs, wc_ref[...], preferred_element_type=F32)
        for d in range(2):
            u = (acc_ref[:, 384 * d : 384 * d + 384] + bc_ref[...]).astype(BF16)
            u_ref[2 * ci + d] = u.reshape(17, 16, 384)
            u = u.astype(F32)
            sq = u * u
            mid = sq[:, 128:256]
            low = jnp.sum(sq[:, 0:128] + jnp.where(lane < 64, mid, 0.0), axis=1, keepdims=True)
            top = jnp.sum(sq[:, 256:384] + jnp.where(lane < 64, 0.0, mid), axis=1, keepdims=True)
            low = lax.rsqrt(low * (1 / 192) + 1e-06)
            top = lax.rsqrt(top * (1 / 192) + 1e-06)
            low = jnp.broadcast_to(low, (272, 128))
            top = jnp.broadcast_to(top, (272, 128))
            scale = jnp.concatenate([low, jnp.where(lane < 64, low, top), top], axis=1)
            r = silu(u * scale * g2_ref[...]).reshape(17, 16, 384)
            frame = iota((1, 16, 384), 1)
            r_ref[2, 2 * ci + d] = r.astype(BF16)
            for shift in (1, 2):
                moved = jnp.where(frame >= shift, pltpu.roll(r, shift, 1), 0.0)
                r_ref[2 - shift, 2 * ci + d] = moved.astype(BF16)
        return carry

    lax.fori_loop(0, 5, corners, 0)

    @pl.when(t == 0)
    def _():
        for d in range(3):
            r_ref[d, 0] = jnp.zeros((17, 16, 384), BF16)

    @pl.when(t == lax.axis_size("tile") - 1)
    def _():
        for d in range(3):
            r_ref[d, 9] = jnp.zeros((17, 16, 384), BF16)

    wide = iota((1, 1, 384), 2)

    @pl.when(s == 0)
    def _():
        for d in range(3):
            r_ref[d, :, 0] = jnp.where(wide < 192, r_ref[d, :, 0].astype(F32), 0.0).astype(BF16)

    @pl.when(s == lax.axis_size("seq") - 1)
    def _():
        for d in range(3):
            r_ref[d, :, 16] = jnp.where(wide < 192, 0.0, r_ref[d, :, 16].astype(F32)).astype(BF16)

    def residual(y, carry):
        even, odd = [], []
        for d in range(3):
            for e in range(3):
                even.append(r_ref[d, y + e, pl.ds(0, 16), :, :].reshape(256, 384))
                even.append(r_ref[d, y + e, pl.ds(1, 16), :, 128:384].reshape(256, 256))
                odd.append(r_ref[d, y + e, pl.ds(0, 16), :, 0:256].reshape(256, 256))
                odd.append(r_ref[d, y + e, pl.ds(1, 16), :, :].reshape(256, 384))
        p = jnp.dot(jnp.concatenate(even, axis=1), w0_ref[...], preferred_element_type=F32)
        q = jnp.dot(jnp.concatenate(odd, axis=1), wp_ref[...], preferred_element_type=F32)
        left = u_ref[y + 1, pl.ds(0, 16)].reshape(256, 384).astype(F32)
        right = u_ref[y + 1, pl.ds(1, 16)].reshape(256, 384).astype(F32)
        b3 = b3_ref[...]
        at = pl.ds(pl.multiple_of(y * 256, 256), 256)
        fin_ref[0, at, :] = p[:, 0:128] + b3[:, 0:128] + left[:, 0:128]
        fin_ref[1, at, :] = (
            p[:, 128:256] + q[:, 0:128] + b3[:, 128:256]
            + jnp.where(lane < 64, left[:, 128:256], right[:, 128:256])
        )
        fin_ref[2, at, :] = q[:, 128:256] + b3[:, 256:384] + right[:, 256:384]
        return carry

    lax.fori_loop(0, 8, residual, 0)

    def finish(f, carry):
        for m in range(16):
            for c in range(3):
                rows = fin_ref[c, pl.ds(m * 16 + f, 8, stride=256), :]
                out_ref[f, :, 384 * m + 128 * c : 384 * m + 128 * c + 128] = rows.astype(BF16)
        return carry

    lax.fori_loop(0, 16, finish, 0)


def first_weights(w_in):
    w = w_in.reshape(3, 3, 48, 384).transpose(1, 0, 2, 3)
    return jnp.pad(w, ((0, 0), (0, 1), (0, 16), (0, 0))).reshape(768, 384)


def corner_weights(w_up):
    w = w_up.reshape(3, 3, 384, 192).astype(F32)
    rows = [[w[0] + w[1], w[2]], [w[0], w[1] + w[2]]]

    def columns(v):
        return [[v[0] + v[1], v[2]], [v[0], v[1] + v[2]]]

    blocks = []
    for r in range(2):
        for c in range(2):
            across = [columns(rows[dy][r])[dx][c] for dy in range(2) for dx in (1, 0)]
            blocks.append(jnp.concatenate(across, axis=1))
    return jnp.concatenate(blocks, axis=0).astype(BF16)


def residual_weights(w_res):
    w = w_res.reshape(9, 3, 192, 192)
    zero = jnp.zeros((9, 64, 192), w.dtype)
    even = jnp.concatenate([w[:, 1], w[:, 0], zero, w[:, 2]], axis=1).reshape(5760, 192)
    odd = jnp.concatenate([w[:, 0], zero, w[:, 2], w[:, 1]], axis=1).reshape(5760, 192)
    return jnp.pad(even, ((0, 0), (0, 64))), jnp.pad(odd, ((0, 0), (64, 0)))


VMEM_SPEC = pl.BlockSpec(memory_space=pltpu.VMEM)


def local(latents, grid_slot, w_in, b_in, gain_in, w_up, b_up, gain_res, w_res, b_res):
    outbox = pl.pallas_call(
        outbox_kernel,
        out_shape=jax.ShapeDtypeStruct((1024, 128), BF16),
        in_specs=[VMEM_SPEC] * 2,
        out_specs=VMEM_SPEC,
        name="outbox",
    )(grid_slot.reshape(1, 128), latents)
    inbox = lax.all_to_all(
        outbox.reshape(128, 8, 128), ("seq", "tile"), split_axis=0, concat_axis=0, tiled=True
    )
    routed = pl.pallas_call(
        route_kernel,
        out_shape=jax.ShapeDtypeStruct((512, 128), BF16),
        in_specs=[VMEM_SPEC],
        out_specs=VMEM_SPEC,
        name="route",
    )(inbox.reshape(1024, 128))
    recv = lax.all_to_all(
        routed.reshape(8, 64, 128), "seq", split_axis=0, concat_axis=0, tiled=True
    ).reshape(512, 128)

    w0, wp = residual_weights(w_res)
    return pl.pallas_call(
        decode_kernel,
        out_shape=jax.ShapeDtypeStruct((16, 8, 6144), BF16),
        in_specs=[VMEM_SPEC] * 10,
        out_specs=VMEM_SPEC,
        scratch_shapes=[
            pltpu.VMEM((3, 8, 4, 16, 128), F32),
            pltpu.VMEM((8, 18, 16, 256), BF16),
            pltpu.VMEM((6, 18, 16, 384), BF16),
            pltpu.VMEM((10, 17, 16, 384), BF16),
            pltpu.VMEM((272, 768), F32),
            pltpu.VMEM((3, 10, 17, 16, 384), BF16),
            pltpu.VMEM((3, 2048, 128), F32),
        ],
        compiler_params=pltpu.CompilerParams(vmem_limit_bytes=56 * 1024 * 1024),
        name="decode",
    )(
        recv,
        first_weights(w_in),
        b_in.reshape(1, 384),
        gain_in.reshape(1, 384),
        corner_weights(w_up),
        jnp.tile(b_up, 2).reshape(1, 384),
        jnp.tile(gain_res, 2).reshape(1, 384),
        w0,
        wp,
        jnp.tile(b_res, 2).reshape(1, 384),
    )


def solution(mesh):
    return jax.shard_map(
        local,
        mesh=mesh,
        in_specs=(P(("seq", "tile"), None), P(("seq", "tile"))) + (P(),) * 8,
        out_specs=P(None, "tile", "seq"),
        check_vma=False,
    )
```

```python
import jax
import jax.numpy as jnp
from jax import lax
from jax.experimental import pallas as pl
from jax.experimental.pallas import tpu as pltpu
from jax.sharding import PartitionSpec as P

F32 = jnp.float32
BF16 = jnp.bfloat16
I32 = jnp.int32
MC = 2


def iota(shape, dim):
    return lax.broadcasted_iota(I32, shape, dim)


def ones_where(cond):
    return jnp.where(cond, 1.0, 0.0).astype(BF16)


def outbox_kernel(slot_ref, lat_ref, out_ref):
    n = 128
    row = jnp.broadcast_to(slot_ref[...], (n, n))
    col = jnp.transpose(row)
    i, j = iota((n, n), 0), iota((n, n), 1)
    same = (row >> 7) == (col >> 7)
    rank_row = jnp.sum(jnp.where(same & (i < j), 1, 0), axis=0, keepdims=True)
    rank_col = jnp.sum(jnp.where(same & (j < i), 1, 0), axis=1, keepdims=True)

    def keys(slot, rank):
        target = slot >> 7
        band = target & 15
        frame, high, group = (slot >> 6) & 1, (slot >> 4) & 3, slot & 15
        upper = high < 2
        halo_target = jnp.where(upper, target - 1, target + 1)
        inside = (upper & (band > 0)) | ((high >= 2) & (band < 15))
        halo_target = jnp.where(inside, halo_target, -1000)
        halo_slot = jnp.where(upper, 4, 2) + rank
        own_label = (frame * 8 + high + 2) * 16 + group + 1
        halo_label = (frame * 8 + jnp.where(upper, high + 6, high - 2)) * 16 + group + 1
        return target, halo_target, halo_slot, own_label, halo_label

    target, halo_target, halo_slot, _, _ = keys(slot_ref[...], rank_row)
    _, _, halo_slot_col, own_label, halo_label = keys(col, rank_col)
    own_table = jnp.where(j == rank_col, own_label, 0).astype(F32).astype(BF16)
    halo_table = jnp.where(j == halo_slot_col, halo_label, 0).astype(F32).astype(BF16)

    q = iota((8 * n, n), 0)
    pick = ones_where((q == target * 8 + rank_row) | (q == halo_target * 8 + halo_slot))
    pick_own = ones_where(q == target * 8 + 6)
    pick_halo = ones_where(q == halo_target * 8 + 6)
    out = jnp.dot(pick, lat_ref[...], preferred_element_type=F32)
    out += jnp.dot(pick_own, own_table, preferred_element_type=F32)
    out += jnp.dot(pick_halo, halo_table, preferred_element_type=F32)
    out_ref[...] = out.astype(BF16)


def route_kernel(inbox_ref, out_ref):
    rows = inbox_ref.shape[0]
    inbox = inbox_ref[...]
    boxes = inbox.astype(F32).reshape(rows // 8, 8, 128)
    labels = jnp.broadcast_to(boxes[:, 6:7, :], boxes.shape)
    slot, lane = iota(boxes.shape, 1), iota(boxes.shape, 2)
    label = jnp.sum(jnp.where((slot == lane) & (slot < 6), labels, 0.0), axis=2, keepdims=True)
    label = label.reshape(rows, 1).astype(I32)
    k = iota((1, 512), 1)
    group = 2 * (k >> 6) - 1 + ((k >> 1) & 3)
    wanted = ((k & 1) * 8 + ((k >> 3) & 7)) * 16 + group + 1
    wanted = jnp.where((group >= 0) & (group < 16), wanted, -1)
    pick = ones_where(label == wanted)
    out = lax.dot_general(pick, inbox, (((0,), (0,)), ((), ())), preferred_element_type=F32)
    out_ref[...] = out.astype(BF16)


def dot_nt(x, w):
    return lax.dot_general(x, w, (((1,), (1,)), ((), ())), preferred_element_type=F32)


def silu(v):
    half = 0.5 * v
    return half * jnp.tanh(half) + half


def decode_kernel(
    recv_ref, w1_ref, wc_hbm, w0_hbm, wp_hbm, vec_ref, out_ref,
    grid_ref, x_ref, a_ref, u_ref, r_ref, fin_ref, wc_ref, w0_ref, wp_ref, sems,
):
    s = lax.axis_index("seq")
    t = lax.axis_index("tile")
    wc_copy = pltpu.make_async_copy(wc_hbm, wc_ref, sems.at[0])
    w0_copy = pltpu.make_async_copy(w0_hbm, w0_ref, sems.at[1])
    wp_copy = pltpu.make_async_copy(wp_hbm, wp_ref, sems.at[2])
    wc_copy.start()
    w0_copy.start()
    wp_copy.start()
    b1, g1, bc, g2, b3 = (vec_ref[n : n + 1, :] for n in range(5))
    lane = iota((1, 128), 1)

    i, k = iota((1536, 512), 0), iota((1536, 512), 1)
    key_i = ((i >> 4) & 31) * 32 + (i & 15) - 2 + (i >> 9)
    key_k = ((k >> 1) & 31) * 32 + 2 * (k >> 6) + (k & 1)
    grid_ref[...] = jnp.dot(
        ones_where(key_i == key_k), recv_ref[...], preferred_element_type=F32
    ).reshape(3, 8, 4, 16, 128)

    def windows(y, carry):
        tiles = [[grid_ref[d, y, c] for c in range(4)] for d in range(3)]
        for ix in range(18):
            c, o = divmod((ix + 6) * 16, 128)

            def window(d, to):
                tile = tiles[d][c]
                if o + 48 > 128:
                    tile = jnp.where(lane >= o, tile, tiles[d][c + 1])
                shift = (to - o) % 128
                return pltpu.roll(tile, shift, 1) if shift else tile

            x_ref[y, ix, :, 0:128] = jnp.where(lane < 64, window(0, 0), window(1, 64)).astype(BF16)
            x_ref[y, ix, :, 128:256] = window(2, 0).astype(BF16)
        return carry

    lax.fori_loop(0, 8, windows, 0)

    def first(iy, carry):
        lhs = jnp.concatenate([x_ref[iy + d].reshape(288, 256) for d in range(3)], axis=1)
        v = jnp.dot(lhs, w1_ref[...], preferred_element_type=F32) + b1
        scale = lax.rsqrt(jnp.mean(v * v, axis=1, keepdims=True) + 1e-06)
        a_ref[iy] = silu(v * scale * g1).astype(BF16).reshape(18, 16, 384)
        return carry

    lax.fori_loop(0, 6, first, 0, unroll=2)

    @pl.when(t == 0)
    def _():
        a_ref[0] = jnp.zeros((18, 16, 384), BF16)

    @pl.when(t == lax.axis_size("tile") - 1)
    def _():
        a_ref[5] = jnp.zeros((18, 16, 384), BF16)

    @pl.when(s == 0)
    def _():
        a_ref[:, 0] = jnp.zeros((6, 16, 384), BF16)

    @pl.when(s == lax.axis_size("seq") - 1)
    def _():
        a_ref[:, 17] = jnp.zeros((6, 16, 384), BF16)

    wc_copy.wait()

    def corners(ci, carry):
        lhs = jnp.concatenate(
            [a_ref[ci + d, pl.ds(e, 17)].reshape(272, 384) for d in range(2) for e in range(2)],
            axis=1,
        )
        acc = dot_nt(lhs, wc_ref[...])
        for d in range(2):
            u = (acc[:, 384 * d : 384 * d + 384] + bc).astype(BF16)
            u_ref[2 * ci + d] = u.reshape(17, 16, 384)
            u = u.astype(F32)
            sq = u * u
            mid = sq[:, 128:256]
            low = jnp.sum(sq[:, 0:128] + jnp.where(lane < 64, mid, 0.0), axis=1, keepdims=True)
            top = jnp.sum(sq[:, 256:384] + jnp.where(lane < 64, 0.0, mid), axis=1, keepdims=True)
            low = lax.rsqrt(low * (1 / 192) + 1e-06)
            top = lax.rsqrt(top * (1 / 192) + 1e-06)
            low = jnp.broadcast_to(low, (272, 128))
            top = jnp.broadcast_to(top, (272, 128))
            scale = jnp.concatenate([low, jnp.where(lane < 64, low, top), top], axis=1)
            r = silu(u * scale * g2).reshape(17, 16, 384)
            frame = iota((1, 16, 384), 1)
            r_ref[2, 2 * ci + d] = r.astype(BF16)
            for shift in (1, 2):
                moved = jnp.where(frame >= shift, pltpu.roll(r, shift, 1), 0.0)
                r_ref[2 - shift, 2 * ci + d] = moved.astype(BF16)
        return carry

    lax.fori_loop(0, 5, corners, 0, unroll=True)

    @pl.when(t == 0)
    def _():
        for d in range(3):
            r_ref[d, 0] = jnp.zeros((17, 16, 384), BF16)

    @pl.when(t == lax.axis_size("tile") - 1)
    def _():
        for d in range(3):
            r_ref[d, 9] = jnp.zeros((17, 16, 384), BF16)

    wide = iota((1, 1, 384), 2)

    @pl.when(s == 0)
    def _():
        for d in range(3):
            r_ref[d, :, 0] = jnp.where(wide < 192, r_ref[d, :, 0].astype(F32), 0.0).astype(BF16)

    @pl.when(s == lax.axis_size("seq") - 1)
    def _():
        for d in range(3):
            r_ref[d, :, 16] = jnp.where(wide < 192, 0.0, r_ref[d, :, 16].astype(F32)).astype(BF16)

    def residual(i, carry):
        m = i * MC
        R = MC * 128
        even, odd = [], []
        for d in range(3):
            for e in range(3):
                def tap(o, lo, hi):
                    return jnp.concatenate([r_ref[d, pl.ds(e, 8), m + o + k, :, lo:hi].reshape(128, hi - lo) for k in range(MC)], axis=0)
                even.append(tap(0, 0, 384)); even.append(tap(1, 128, 384))
                odd.append(tap(0, 0, 256)); odd.append(tap(1, 0, 384))
        p = dot_nt(jnp.concatenate(even, axis=1), w0_ref[...])
        q = dot_nt(jnp.concatenate(odd, axis=1), wp_ref[...])
        slot = i & 1
        for k in range(MC):
            left = u_ref[pl.ds(1, 8), m + k].reshape(128, 384).astype(F32)
            right = u_ref[pl.ds(1, 8), m + k + 1].reshape(128, 384).astype(F32)
            pk = p[128 * k : 128 * k + 128]
            qk = q[128 * k : 128 * k + 128]
            fin_ref[slot, k, 0] = pk[:, 0:128] + b3[:, 0:128] + left[:, 0:128]
            fin_ref[slot, k, 1] = (
                pk[:, 128:256] + qk[:, 0:128] + b3[:, 128:256]
                + jnp.where(lane < 64, left[:, 128:256], right[:, 128:256])
            )
            fin_ref[slot, k, 2] = qk[:, 128:256] + b3[:, 256:384] + right[:, 256:384]
        finish(i - 1, 1 - slot)
        return carry

    def finish(i, slot):
        i = jnp.maximum(i, 0)
        for k in range(MC):
            for c in range(3):
                for f in range(16):
                    rows = fin_ref[slot, k, c, pl.ds(f, 8, stride=16), :]
                    at = pl.multiple_of((i * MC + k) * 384 + c * 128, 128)
                    out_ref[f, :, pl.ds(at, 128)] = rows.astype(BF16)

    w0_copy.wait()
    wp_copy.wait()
    lax.fori_loop(0, 16 // MC, residual, 0)
    finish(16 // MC - 1, (16 // MC - 1) & 1)


def prepare_kernel(
    win_ref, wup_ref, wres_ref, bin_ref, gin_ref, bup_ref, gres_ref, bres_ref,
    w1_ref, wc_ref, w0_ref, wp_ref, vec_ref,
):
    for row in range(3):
        for time in range(3):
            at = row * 256 + time * 64
            w1_ref[at : at + 48] = win_ref[(time * 3 + row) * 48 : (time * 3 + row) * 48 + 48]
            w1_ref[at + 48 : at + 64] = jnp.zeros((16, 384), BF16)
        w1_ref[row * 256 + 192 : row * 256 + 256] = jnp.zeros((64, 384), BF16)

    taps = [[[0, 1], [2]], [[0], [1, 2]]]
    for dy in range(2):
        for place, dx in enumerate((1, 0)):
            for r in range(2):
                for c in range(2):
                    total = None
                    for b in taps[dy][r]:
                        for e in taps[dx][c]:
                            at = (b * 3 + e) * 384
                            term = wup_ref[:, at : at + 384].astype(F32)
                            total = term if total is None else total + term
                    at = (r * 2 + c) * 384
                    to = (dy * 2 + place) * 192
                    wc_ref[to : to + 192, at : at + 384] = total.astype(BF16)

    zero = jnp.zeros((192, 64), BF16)
    for tap in range(9):
        w = [wres_ref[:, (tap * 3 + e) * 192 : (tap * 3 + e) * 192 + 192] for e in range(3)]
        at = slice(tap * 640, tap * 640 + 640)
        w0_ref[0:192, at] = jnp.concatenate([w[1], w[0], zero, w[2]], axis=1)
        wp_ref[64:256, at] = jnp.concatenate([w[0], zero, w[2], w[1]], axis=1)
    w0_ref[192:256, :] = jnp.zeros((64, 5760), BF16)
    wp_ref[0:64, :] = jnp.zeros((64, 5760), BF16)

    vec_ref[...] = jnp.zeros((8, 384), F32)
    for row, ref in enumerate((bin_ref, gin_ref)):
        vec_ref[row : row + 1, :] = ref[...].reshape(1, 384)
    for row, ref in enumerate((bup_ref, gres_ref, bres_ref)):
        v = ref[...].reshape(1, 192)
        vec_ref[row + 2 : row + 3, :] = jnp.concatenate([v, v], axis=1)


VMEM_SPEC = pl.BlockSpec(memory_space=pltpu.VMEM)
ANY_SPEC = pl.BlockSpec(memory_space=pl.ANY)


def local(latents, grid_slot, w_in, b_in, gain_in, w_up, b_up, gain_res, w_res, b_res):
    outbox = pl.pallas_call(
        outbox_kernel,
        out_shape=jax.ShapeDtypeStruct((1024, 128), BF16),
        in_specs=[VMEM_SPEC] * 2,
        out_specs=VMEM_SPEC,
        name="outbox",
    )(grid_slot.reshape(1, 128), latents)
    inbox = lax.all_to_all(
        outbox.reshape(128, 8, 128), ("seq", "tile"), split_axis=0, concat_axis=0, tiled=True
    )
    prepared = pl.pallas_call(
        prepare_kernel,
        out_shape=[
            jax.ShapeDtypeStruct((768, 384), BF16),
            jax.ShapeDtypeStruct((768, 1536), BF16),
            jax.ShapeDtypeStruct((256, 5760), BF16),
            jax.ShapeDtypeStruct((256, 5760), BF16),
            jax.ShapeDtypeStruct((8, 384), F32),
        ],
        in_specs=[VMEM_SPEC] * 8,
        out_specs=[VMEM_SPEC] * 5,
        cost_estimate=pl.CostEstimate(flops=10_000_000, bytes_accessed=16_000_000, transcendentals=0),
        compiler_params=pltpu.CompilerParams(vmem_limit_bytes=32 * 1024 * 1024),
        name="prepare",
    )(w_in, w_up.T, w_res.T, b_in, gain_in, b_up, gain_res, b_res)
    routed = pl.pallas_call(
        route_kernel,
        out_shape=jax.ShapeDtypeStruct((512, 128), BF16),
        in_specs=[VMEM_SPEC],
        out_specs=VMEM_SPEC,
        name="route",
    )(inbox.reshape(1024, 128))
    recv = lax.all_to_all(
        routed.reshape(8, 64, 128), "seq", split_axis=0, concat_axis=0, tiled=True
    ).reshape(512, 128)
    return decode(recv, *prepared)


def decode(recv, w1, wc, w0, wp, vec):
    return pl.pallas_call(
        decode_kernel,
        out_shape=jax.ShapeDtypeStruct((16, 8, 6144), BF16),
        in_specs=[VMEM_SPEC] * 2 + [ANY_SPEC] * 3 + [VMEM_SPEC],
        out_specs=VMEM_SPEC,
        scratch_shapes=[
            pltpu.VMEM((3, 8, 4, 16, 128), F32),
            pltpu.VMEM((8, 18, 16, 256), BF16),
            pltpu.VMEM((6, 18, 16, 384), BF16),
            pltpu.VMEM((10, 17, 16, 384), BF16),
            pltpu.VMEM((3, 10, 17, 16, 384), BF16),
            pltpu.VMEM((2, MC, 3, 128, 128), F32),
            pltpu.VMEM((768, 1536), BF16),
            pltpu.VMEM((256, 5760), BF16),
            pltpu.VMEM((256, 5760), BF16),
            pltpu.SemaphoreType.DMA((3,)),
        ],
        compiler_params=pltpu.CompilerParams(vmem_limit_bytes=48 * 1024 * 1024),
        name="decode",
    )(recv, w1, wc, w0, wp, vec)


def solution(mesh):
    return jax.shard_map(
        local,
        mesh=mesh,
        in_specs=(P(("seq", "tile"), None), P(("seq", "tile"))) + (P(),) * 8,
        out_specs=P(None, "tile", "seq"),
        check_vma=False,
    )
```

```python
import jax
import jax.numpy as jnp
from jax import lax
from jax.experimental import pallas as pl
from jax.experimental.pallas import tpu as pltpu
from jax.sharding import PartitionSpec as P

F32 = jnp.float32
BF16 = jnp.bfloat16
I32 = jnp.int32
MC = 2


def iota(shape, dim):
    return lax.broadcasted_iota(I32, shape, dim)


def ones_where(cond):
    return jnp.where(cond, 1.0, 0.0).astype(BF16)


def outbox_kernel(slot_ref, lat_ref, out_ref):
    n = 128
    row = jnp.broadcast_to(slot_ref[...], (n, n))
    col = jnp.transpose(row)
    i, j = iota((n, n), 0), iota((n, n), 1)
    same = (row >> 7) == (col >> 7)
    rank_row = jnp.sum(jnp.where(same & (i < j), 1, 0), axis=0, keepdims=True)
    rank_col = jnp.sum(jnp.where(same & (j < i), 1, 0), axis=1, keepdims=True)

    def keys(slot, rank):
        target = slot >> 7
        band = target & 15
        frame, high, group = (slot >> 6) & 1, (slot >> 4) & 3, slot & 15
        upper = high < 2
        halo_target = jnp.where(upper, target - 1, target + 1)
        inside = (upper & (band > 0)) | ((high >= 2) & (band < 15))
        halo_target = jnp.where(inside, halo_target, -1000)
        halo_slot = jnp.where(upper, 4, 2) + rank
        own_label = (frame * 8 + high + 2) * 16 + group + 1
        halo_label = (frame * 8 + jnp.where(upper, high + 6, high - 2)) * 16 + group + 1
        return target, halo_target, halo_slot, own_label, halo_label

    target, halo_target, halo_slot, _, _ = keys(slot_ref[...], rank_row)
    _, _, halo_slot_col, own_label, halo_label = keys(col, rank_col)
    own_table = jnp.where(j == rank_col, own_label, 0).astype(F32).astype(BF16)
    halo_table = jnp.where(j == halo_slot_col, halo_label, 0).astype(F32).astype(BF16)

    q = iota((8 * n, n), 0)
    pick = ones_where((q == target * 8 + rank_row) | (q == halo_target * 8 + halo_slot))
    pick_own = ones_where(q == target * 8 + 6)
    pick_halo = ones_where(q == halo_target * 8 + 6)
    out = jnp.dot(pick, lat_ref[...], preferred_element_type=F32)
    out += jnp.dot(pick_own, own_table, preferred_element_type=F32)
    out += jnp.dot(pick_halo, halo_table, preferred_element_type=F32)
    out_ref[...] = out.astype(BF16)


def route_kernel(inbox_ref, after_ref, out_ref):
    rows = inbox_ref.shape[0]
    inbox = inbox_ref[...]
    boxes = inbox.astype(F32).reshape(rows // 8, 8, 128)
    labels = jnp.broadcast_to(boxes[:, 6:7, :], boxes.shape)
    slot, lane = iota(boxes.shape, 1), iota(boxes.shape, 2)
    label = jnp.sum(jnp.where((slot == lane) & (slot < 6), labels, 0.0), axis=2, keepdims=True)
    label = label.reshape(rows, 1).astype(I32)
    k = iota((1, 512), 1)
    group = 2 * (k >> 6) - 1 + ((k >> 1) & 3)
    wanted = ((k & 1) * 8 + ((k >> 3) & 7)) * 16 + group + 1
    wanted = jnp.where((group >= 0) & (group < 16), wanted, -1)
    pick = ones_where(label == wanted)
    out = lax.dot_general(pick, inbox, (((0,), (0,)), ((), ())), preferred_element_type=F32)
    out_ref[...] = out.astype(BF16)


def dot_nt(x, w):
    return lax.dot_general(x, w, (((1,), (1,)), ((), ())), preferred_element_type=F32)


def silu(v):
    half = 0.5 * v
    return half * jnp.tanh(half) + half


def decode_kernel(
    recv_ref, w1_ref, wc_hbm, w0_hbm, wp_hbm, vec_ref, out_ref,
    grid_ref, x_ref, a_ref, u_ref, r_ref, fin_ref, wc_ref, w0_ref, wp_ref, sems,
):
    s = lax.axis_index("seq")
    t = lax.axis_index("tile")
    wc_copy = pltpu.make_async_copy(wc_hbm, wc_ref, sems.at[0])
    w0_copy = pltpu.make_async_copy(w0_hbm, w0_ref, sems.at[1])
    wp_copy = pltpu.make_async_copy(wp_hbm, wp_ref, sems.at[2])
    wc_copy.start()
    w0_copy.start()
    wp_copy.start()
    b1, g1, bc, g2, b3 = (vec_ref[n : n + 1, :] for n in range(5))
    lane = iota((1, 128), 1)

    i, k = iota((1536, 512), 0), iota((1536, 512), 1)
    key_i = ((i >> 4) & 31) * 32 + (i & 15) - 2 + (i >> 9)
    key_k = ((k >> 1) & 31) * 32 + 2 * (k >> 6) + (k & 1)
    grid_ref[...] = jnp.dot(
        ones_where(key_i == key_k), recv_ref[...], preferred_element_type=F32
    ).reshape(3, 8, 4, 16, 128)

    def windows(y, carry):
        tiles = [[grid_ref[d, y, c] for c in range(4)] for d in range(3)]
        for ix in range(18):
            c, o = divmod((ix + 6) * 16, 128)

            def window(d, to):
                tile = tiles[d][c]
                if o + 48 > 128:
                    tile = jnp.where(lane >= o, tile, tiles[d][c + 1])
                shift = (to - o) % 128
                return pltpu.roll(tile, shift, 1) if shift else tile

            x_ref[y, ix, :, 0:128] = jnp.where(lane < 64, window(0, 0), window(1, 64)).astype(BF16)
            x_ref[y, ix, :, 128:256] = window(2, 0).astype(BF16)
        return carry

    lax.fori_loop(0, 8, windows, 0)

    def first(iy, carry):
        lhs = jnp.concatenate([x_ref[iy + d].reshape(288, 256) for d in range(3)], axis=1)
        v = jnp.dot(lhs, w1_ref[...], preferred_element_type=F32) + b1
        scale = lax.rsqrt(jnp.mean(v * v, axis=1, keepdims=True) + 1e-06)
        a_ref[iy] = silu(v * scale * g1).astype(BF16).reshape(18, 16, 384)
        return carry

    lax.fori_loop(0, 6, first, 0, unroll=2)

    @pl.when(t == 0)
    def _():
        a_ref[0] = jnp.zeros((18, 16, 384), BF16)

    @pl.when(t == lax.axis_size("tile") - 1)
    def _():
        a_ref[5] = jnp.zeros((18, 16, 384), BF16)

    @pl.when(s == 0)
    def _():
        a_ref[:, 0] = jnp.zeros((6, 16, 384), BF16)

    @pl.when(s == lax.axis_size("seq") - 1)
    def _():
        a_ref[:, 17] = jnp.zeros((6, 16, 384), BF16)


    wc_copy.wait()

    def corners(ci, carry):
        lhs = jnp.concatenate(
            [a_ref[ci + d, pl.ds(e, 17)].reshape(272, 384) for d in range(2) for e in range(2)],
            axis=1,
        )
        acc = dot_nt(lhs, wc_ref[...])
        for d in range(2):
            u = (acc[:, 384 * d : 384 * d + 384] + bc).astype(BF16)
            u_ref[2 * ci + d] = u.reshape(17, 16, 384)
            u = u.astype(F32)
            sq = u * u
            mid = sq[:, 128:256]
            low = jnp.sum(sq[:, 0:128] + jnp.where(lane < 64, mid, 0.0), axis=1, keepdims=True)
            top = jnp.sum(sq[:, 256:384] + jnp.where(lane < 64, 0.0, mid), axis=1, keepdims=True)
            low = lax.rsqrt(low * (1 / 192) + 1e-06)
            top = lax.rsqrt(top * (1 / 192) + 1e-06)
            low = jnp.broadcast_to(low, (272, 128))
            top = jnp.broadcast_to(top, (272, 128))
            scale = jnp.concatenate([low, jnp.where(lane < 64, low, top), top], axis=1)
            r = silu(u * scale * g2).reshape(17, 16, 384)
            frame = iota((1, 16, 384), 1)
            r_ref[2, 2 * ci + d] = r.astype(BF16)
            for shift in (1, 2):
                moved = jnp.where(frame >= shift, pltpu.roll(r, shift, 1), 0.0)
                r_ref[2 - shift, 2 * ci + d] = moved.astype(BF16)
        return carry

    lax.fori_loop(0, 5, corners, 0, unroll=True)

    @pl.when(t == 0)
    def _():
        for d in range(3):
            r_ref[d, 0] = jnp.zeros((17, 16, 384), BF16)

    @pl.when(t == lax.axis_size("tile") - 1)
    def _():
        for d in range(3):
            r_ref[d, 9] = jnp.zeros((17, 16, 384), BF16)

    wide = iota((1, 1, 384), 2)

    @pl.when(s == 0)
    def _():
        for d in range(3):
            r_ref[d, :, 0] = jnp.where(wide < 192, r_ref[d, :, 0].astype(F32), 0.0).astype(BF16)

    @pl.when(s == lax.axis_size("seq") - 1)
    def _():
        for d in range(3):
            r_ref[d, :, 16] = jnp.where(wide < 192, 0.0, r_ref[d, :, 16].astype(F32)).astype(BF16)

    def residual(i, carry):
        m = i * MC
        R = MC * 128
        even, odd = [], []
        for d in range(3):
            for e in range(3):
                def tap(o, lo, hi):
                    return jnp.concatenate([r_ref[d, pl.ds(e, 8), m + o + k, :, lo:hi].reshape(128, hi - lo) for k in range(MC)], axis=0)
                even.append(tap(0, 0, 384)); even.append(tap(1, 128, 384))
                odd.append(tap(0, 0, 256)); odd.append(tap(1, 0, 384))
        p = dot_nt(jnp.concatenate(even, axis=1), w0_ref[...])
        q = dot_nt(jnp.concatenate(odd, axis=1), wp_ref[...])
        slot = i & 1
        for k in range(MC):
            left = u_ref[pl.ds(1, 8), m + k].reshape(128, 384).astype(F32)
            right = u_ref[pl.ds(1, 8), m + k + 1].reshape(128, 384).astype(F32)
            pk = p[128 * k : 128 * k + 128]
            qk = q[128 * k : 128 * k + 128]
            fin_ref[slot, k, 0] = pk[:, 0:128] + b3[:, 0:128] + left[:, 0:128]
            fin_ref[slot, k, 1] = (
                pk[:, 128:256] + qk[:, 0:128] + b3[:, 128:256]
                + jnp.where(lane < 64, left[:, 128:256], right[:, 128:256])
            )
            fin_ref[slot, k, 2] = qk[:, 128:256] + b3[:, 256:384] + right[:, 256:384]
        finish(i - 1, 1 - slot)
        return carry

    def finish(i, slot):
        i = jnp.maximum(i, 0)
        for k in range(MC):
            for c in range(3):
                for f in range(16):
                    rows = fin_ref[slot, k, c, pl.ds(f, 8, stride=16), :]
                    at = pl.multiple_of((i * MC + k) * 384 + c * 128, 128)
                    out_ref[f, :, pl.ds(at, 128)] = rows.astype(BF16)

    w0_copy.wait()
    wp_copy.wait()
    lax.fori_loop(0, 16 // MC, residual, 0)
    finish(16 // MC - 1, (16 // MC - 1) & 1)


def prepare_kernel(
    win_hbm, wup_hbm, wres_hbm, bin_hbm, gin_hbm, bup_hbm, gres_hbm, bres_hbm,
    w1_ref, wc_hbm, w0_hbm, wp_hbm, vec_ref,
    win_ref, wup_ref, wres_ref, bin_ref, gin_ref, bup_ref, gres_ref, bres_ref,
    wc_ref, w0_ref, wp_ref, sems, out_sems,
):
    pairs = (
        (wup_hbm, wup_ref), (wres_hbm, wres_ref), (win_hbm, win_ref), (bin_hbm, bin_ref),
        (gin_hbm, gin_ref), (bup_hbm, bup_ref), (gres_hbm, gres_ref), (bres_hbm, bres_ref),
    )
    copies = [pltpu.make_async_copy(x, y, sems.at[n]) for n, (x, y) in enumerate(pairs)]
    for copy in copies:
        copy.start()
    copies[0].wait()
    taps = [[[0, 1], [2]], [[0], [1, 2]]]
    for dy in range(2):
        for place, dx in enumerate((1, 0)):
            for r in range(2):
                for c in range(2):
                    total = None
                    for b in taps[dy][r]:
                        for e in taps[dx][c]:
                            at = (b * 3 + e) * 384
                            term = wup_ref[:, at : at + 384].astype(F32)
                            total = term if total is None else total + term
                    at = (r * 2 + c) * 384
                    to = (dy * 2 + place) * 192
                    wc_ref[to : to + 192, at : at + 384] = total.astype(BF16)

    wc_copy = pltpu.make_async_copy(wc_ref, wc_hbm, out_sems.at[0])
    wc_copy.start()
    copies[1].wait()
    zero = jnp.zeros((192, 64), BF16)
    for tap in range(9):
        w = [wres_ref[:, (tap * 3 + e) * 192 : (tap * 3 + e) * 192 + 192] for e in range(3)]
        at = slice(tap * 640, tap * 640 + 640)
        w0_ref[0:192, at] = jnp.concatenate([w[1], w[0], zero, w[2]], axis=1)
        wp_ref[64:256, at] = jnp.concatenate([w[0], zero, w[2], w[1]], axis=1)
    w0_ref[192:256, :] = jnp.zeros((64, 5760), BF16)
    wp_ref[0:64, :] = jnp.zeros((64, 5760), BF16)
    w0_copy = pltpu.make_async_copy(w0_ref, w0_hbm, out_sems.at[1])
    wp_copy = pltpu.make_async_copy(wp_ref, wp_hbm, out_sems.at[2])
    w0_copy.start()
    wp_copy.start()

    for copy in copies[2:]:
        copy.wait()
    for row in range(3):
        for time in range(3):
            at = row * 256 + time * 64
            w1_ref[at : at + 48] = win_ref[(time * 3 + row) * 48 : (time * 3 + row) * 48 + 48]
            w1_ref[at + 48 : at + 64] = jnp.zeros((16, 384), BF16)
        w1_ref[row * 256 + 192 : row * 256 + 256] = jnp.zeros((64, 384), BF16)

    vec_ref[...] = jnp.zeros((8, 384), F32)
    for row, ref in enumerate((bin_ref, gin_ref)):
        vec_ref[row : row + 1, :] = ref[...].reshape(1, 384)
    for row, ref in enumerate((bup_ref, gres_ref, bres_ref)):
        v = ref[...].reshape(1, 192)
        vec_ref[row + 2 : row + 3, :] = jnp.concatenate([v, v], axis=1)
    wc_copy.wait()
    w0_copy.wait()
    wp_copy.wait()


VMEM_SPEC = pl.BlockSpec(memory_space=pltpu.VMEM)
ANY_SPEC = pl.BlockSpec(memory_space=pl.ANY)
HBM_SPEC = pl.BlockSpec(memory_space=pltpu.HBM)


def local(latents, grid_slot, w_in, b_in, gain_in, w_up, b_up, gain_res, w_res, b_res):
    outbox = pl.pallas_call(
        outbox_kernel,
        out_shape=jax.ShapeDtypeStruct((1024, 128), BF16),
        in_specs=[VMEM_SPEC] * 2,
        out_specs=VMEM_SPEC,
        name="outbox",
    )(grid_slot.reshape(1, 128), latents)
    inbox = lax.all_to_all(
        outbox.reshape(128, 8, 128), ("seq", "tile"), split_axis=0, concat_axis=0, tiled=True
    )
    prepared = pl.pallas_call(
        prepare_kernel,
        out_shape=[
            jax.ShapeDtypeStruct((768, 384), BF16),
            pltpu.HBM((768, 1536), BF16),
            pltpu.HBM((256, 5760), BF16),
            pltpu.HBM((256, 5760), BF16),
            jax.ShapeDtypeStruct((8, 384), F32),
        ],
        in_specs=[HBM_SPEC] * 8,
        out_specs=[VMEM_SPEC] + [HBM_SPEC] * 3 + [VMEM_SPEC],
        scratch_shapes=[
            pltpu.VMEM((432, 384), BF16),
            pltpu.VMEM((192, 3456), BF16),
            pltpu.VMEM((192, 5184), BF16),
            pltpu.VMEM((384,), F32),
            pltpu.VMEM((384,), F32),
            pltpu.VMEM((192,), F32),
            pltpu.VMEM((192,), F32),
            pltpu.VMEM((192,), F32),
            pltpu.VMEM((768, 1536), BF16),
            pltpu.VMEM((256, 5760), BF16),
            pltpu.VMEM((256, 5760), BF16),
            pltpu.SemaphoreType.DMA((8,)),
            pltpu.SemaphoreType.DMA((3,)),
        ],
        cost_estimate=pl.CostEstimate(flops=10_000_000, bytes_accessed=16_000_000, transcendentals=0),
        compiler_params=pltpu.CompilerParams(vmem_limit_bytes=28 * 1024 * 1024),
        name="prepare",
    )(
        *(
            pltpu.with_memory_space_constraint(w, pltpu.HBM)
            for w in (w_in, w_up.T, w_res.T, b_in, gain_in, b_up, gain_res, b_res)
        )
    )
    routed = pl.pallas_call(
        route_kernel,
        out_shape=jax.ShapeDtypeStruct((512, 128), BF16),
        in_specs=[VMEM_SPEC, ANY_SPEC],
        out_specs=VMEM_SPEC,
        compiler_params=pltpu.CompilerParams(vmem_limit_bytes=12 * 1024 * 1024),
        name="route",
    )(inbox.reshape(1024, 128), prepared[4])
    recv = lax.all_to_all(
        routed.reshape(8, 64, 128), "seq", split_axis=0, concat_axis=0, tiled=True
    ).reshape(512, 128)
    return decode(recv, *prepared)


def decode(recv, w1, wc, w0, wp, vec):
    return pl.pallas_call(
        decode_kernel,
        out_shape=jax.ShapeDtypeStruct((16, 8, 6144), BF16),
        in_specs=[VMEM_SPEC] * 2 + [HBM_SPEC] * 3 + [VMEM_SPEC],
        out_specs=VMEM_SPEC,
        scratch_shapes=[
            pltpu.VMEM((3, 8, 4, 16, 128), F32),
            pltpu.VMEM((8, 18, 16, 256), BF16),
            pltpu.VMEM((6, 18, 16, 384), BF16),
            pltpu.VMEM((10, 17, 16, 384), BF16),
            pltpu.VMEM((3, 10, 17, 16, 384), BF16),
            pltpu.VMEM((2, MC, 3, 128, 128), F32),
            pltpu.VMEM((768, 1536), BF16),
            pltpu.VMEM((256, 5760), BF16),
            pltpu.VMEM((256, 5760), BF16),
            pltpu.SemaphoreType.DMA((3,)),
        ],
        compiler_params=pltpu.CompilerParams(vmem_limit_bytes=44 * 1024 * 1024),
        name="decode",
    )(recv, w1, *(pltpu.with_memory_space_constraint(w, pltpu.HBM) for w in (wc, w0, wp)), vec)


def solution(mesh):
    return jax.shard_map(
        local,
        mesh=mesh,
        in_specs=(P(("seq", "tile"), None), P(("seq", "tile"))) + (P(),) * 8,
        out_specs=P(None, "tile", "seq"),
        check_vma=False,
    )
```

```python
import jax
import jax.numpy as jnp
from jax import lax
from jax.experimental import pallas as pl
from jax.experimental.pallas import tpu as pltpu
from jax.sharding import PartitionSpec as P

F32 = jnp.float32
BF16 = jnp.bfloat16
I32 = jnp.int32
NI = 8


def iota(shape, dim):
    return lax.broadcasted_iota(I32, shape, dim)


def ones_where(cond):
    return jnp.where(cond, 1.0, 0.0).astype(BF16)


def outbox_kernel(slot_ref, lat_ref, out_ref):
    n = 128
    row = jnp.broadcast_to(slot_ref[...], (n, n))
    col = jnp.transpose(row)
    i, j = iota((n, n), 0), iota((n, n), 1)
    same = (row >> 7) == (col >> 7)
    rank_row = jnp.sum(jnp.where(same & (i < j), 1, 0), axis=0, keepdims=True)
    rank_col = jnp.sum(jnp.where(same & (j < i), 1, 0), axis=1, keepdims=True)

    def keys(slot, rank):
        target = slot >> 7
        band = target & 15
        frame, high, group = (slot >> 6) & 1, (slot >> 4) & 3, slot & 15
        upper = high < 2
        halo_target = jnp.where(upper, target - 1, target + 1)
        inside = (upper & (band > 0)) | ((high >= 2) & (band < 15))
        halo_target = jnp.where(inside, halo_target, -1000)
        halo_slot = jnp.where(upper, 4, 2) + rank
        own_label = (frame * 8 + high + 2) * 16 + group + 1
        halo_label = (frame * 8 + jnp.where(upper, high + 6, high - 2)) * 16 + group + 1
        return target, halo_target, halo_slot, own_label, halo_label

    target, halo_target, halo_slot, _, _ = keys(slot_ref[...], rank_row)
    _, _, halo_slot_col, own_label, halo_label = keys(col, rank_col)
    own_table = jnp.where(j == rank_col, own_label, 0).astype(F32).astype(BF16)
    halo_table = jnp.where(j == halo_slot_col, halo_label, 0).astype(F32).astype(BF16)

    q = iota((8 * n, n), 0)
    pick = ones_where((q == target * 8 + rank_row) | (q == halo_target * 8 + halo_slot))
    pick_own = ones_where(q == target * 8 + 6)
    pick_halo = ones_where(q == halo_target * 8 + 6)
    out = jnp.dot(pick, lat_ref[...], preferred_element_type=F32)
    out += jnp.dot(pick_own, own_table, preferred_element_type=F32)
    out += jnp.dot(pick_halo, halo_table, preferred_element_type=F32)
    out_ref[...] = out.astype(BF16)


def route_kernel(inbox_ref, after_ref, out_ref):
    rows = inbox_ref.shape[0]
    inbox = inbox_ref[...]
    boxes = inbox.astype(F32).reshape(rows // 8, 8, 128)
    labels = jnp.broadcast_to(boxes[:, 6:7, :], boxes.shape)
    slot, lane = iota(boxes.shape, 1), iota(boxes.shape, 2)
    label = jnp.sum(jnp.where((slot == lane) & (slot < 6), labels, 0.0), axis=2, keepdims=True)
    label = label.reshape(rows, 1).astype(I32)
    k = iota((1, 512), 1)
    group = 2 * (k >> 6) - 1 + ((k >> 1) & 3)
    wanted = ((k & 1) * 8 + ((k >> 3) & 7)) * 16 + group + 1
    wanted = jnp.where((group >= 0) & (group < 16), wanted, -1)
    pick = ones_where(label == wanted)
    out = lax.dot_general(pick, inbox, (((0,), (0,)), ((), ())), preferred_element_type=F32)
    out_ref[...] = out.astype(BF16)


def dot_nt(x, w):
    return lax.dot_general(x, w, (((1,), (1,)), ((), ())), preferred_element_type=F32)


def silu(v):
    half = 0.5 * v
    return half * jnp.tanh(half) + half


def decode_kernel(
    recv_ref, w1_ref, wc_hbm, w0_hbm, wp_hbm, vec_ref, out_ref,
    grid_ref, x_ref, a_ref, u_ref, r_ref, fin_ref, wc_ref, w0_ref, wp_ref, sems,
):
    s = lax.axis_index("seq")
    t = lax.axis_index("tile")
    wc_copy = pltpu.make_async_copy(wc_hbm, wc_ref, sems.at[0])
    w0_copy = pltpu.make_async_copy(w0_hbm, w0_ref, sems.at[1])
    wp_copy = pltpu.make_async_copy(wp_hbm, wp_ref.at[pl.ds(64, 192)], sems.at[2])
    wc_copy.start()
    w0_copy.start()
    wp_copy.start()
    b1, g1, bc, g2, b3 = (vec_ref[n : n + 1, :] for n in range(5))
    lane = iota((1, 128), 1)

    i, k = iota((1536, 512), 0), iota((1536, 512), 1)
    key_i = ((i >> 4) & 31) * 32 + 2 * (i & 7) + ((i >> 3) & 1) - 2 + (i >> 9)
    key_k = ((k >> 1) & 31) * 32 + 2 * (k >> 6) + (k & 1)
    grid_ref[...] = jnp.dot(
        ones_where(key_i == key_k), recv_ref[...], preferred_element_type=F32
    ).reshape(3, 8, 4, 16, 128)

    def windows(y, carry):
        tiles = [[grid_ref[d, y, c] for c in range(4)] for d in range(3)]
        for ix in range(18):
            c, o = divmod((ix + 6) * 16, 128)

            def window(d, to):
                tile = tiles[d][c]
                if o + 48 > 128:
                    tile = jnp.where(lane >= o, tile, tiles[d][c + 1])
                shift = (to - o) % 128
                return pltpu.roll(tile, shift, 1) if shift else tile

            x_ref[y, ix, :, 0:128] = jnp.where(lane < 64, window(0, 0), window(1, 64)).astype(BF16)
            x_ref[y, ix, :, 128:256] = window(2, 0).astype(BF16)
        return carry

    lax.fori_loop(0, 8, windows, 0)

    def first(iy, carry):
        lhs = jnp.concatenate([x_ref[iy + d].reshape(288, 256) for d in range(3)], axis=1)
        v = jnp.dot(lhs, w1_ref[...], preferred_element_type=F32) + b1
        scale = lax.rsqrt(jnp.mean(v * v, axis=1, keepdims=True) + 1e-06)
        a_ref[iy] = silu(v * scale * g1).astype(BF16).reshape(18, 16, 384)
        return carry

    lax.fori_loop(0, 6, first, 0, unroll=2)

    @pl.when(t == 0)
    def _():
        a_ref[0] = jnp.zeros((18, 16, 384), BF16)

    @pl.when(t == lax.axis_size("tile") - 1)
    def _():
        a_ref[5] = jnp.zeros((18, 16, 384), BF16)

    @pl.when(s == 0)
    def _():
        a_ref[:, 0] = jnp.zeros((6, 16, 384), BF16)

    @pl.when(s == lax.axis_size("seq") - 1)
    def _():
        a_ref[:, 17] = jnp.zeros((6, 16, 384), BF16)


    wc_copy.wait()

    def corners(ci, carry):
        lhs = jnp.concatenate(
            [a_ref[ci + d, pl.ds(e, 17)].reshape(272, 384) for d in range(2) for e in range(2)],
            axis=1,
        )
        acc = dot_nt(lhs, wc_ref[...])
        for d in range(2):
            u = (acc[:, 384 * d : 384 * d + 384] + bc).astype(BF16)
            u_ref[2 * ci + d] = u.reshape(17, 16, 384)
            u = u.astype(F32)
            sq = u * u
            mid = sq[:, 128:256]
            low = jnp.sum(sq[:, 0:128] + jnp.where(lane < 64, mid, 0.0), axis=1, keepdims=True)
            top = jnp.sum(sq[:, 256:384] + jnp.where(lane < 64, 0.0, mid), axis=1, keepdims=True)
            low = lax.rsqrt(low * (1 / 192) + 1e-06)
            top = lax.rsqrt(top * (1 / 192) + 1e-06)
            low = jnp.broadcast_to(low, (272, 128))
            top = jnp.broadcast_to(top, (272, 128))
            scale = jnp.concatenate([low, jnp.where(lane < 64, low, top), top], axis=1)
            r = silu(u * scale * g2).reshape(17, 16, 384)
            d2, d3 = r[:, 0:8], r[:, 8:16]
            later = iota((1, 8, 384), 1) > 0
            d0 = jnp.where(later, pltpu.roll(d2, 1, 1), 0.0)
            d1 = jnp.where(later, pltpu.roll(d3, 1, 1), 0.0)
            for n, v in enumerate((d0 - d2, d1 + d2, d2 - d1, d1 - d3)):
                r_ref[n, 0, 2 * ci + d] = v[0:16].reshape(8, 16, 384).astype(BF16)
                r_ref[n, 1, 2 * ci + d] = v[1:17].reshape(8, 16, 384).astype(BF16)
        return carry

    lax.fori_loop(0, 5, corners, 0, unroll=True)

    @pl.when(t == 0)
    def _():
        for n in range(4):
            r_ref[n, :, 0] = jnp.zeros((2, 8, 16, 384), BF16)

    @pl.when(t == lax.axis_size("tile") - 1)
    def _():
        for n in range(4):
            r_ref[n, :, 9] = jnp.zeros((2, 8, 16, 384), BF16)

    row, wide = iota((1, 16, 384), 1), iota((1, 16, 384), 2)

    @pl.when(s == 0)
    def _():
        for n in range(4):
            v = r_ref[n, 0, :, 0].astype(F32)
            r_ref[n, 0, :, 0] = jnp.where((wide < 192) | (row >= 8), v, 0.0).astype(BF16)

    @pl.when(s == lax.axis_size("seq") - 1)
    def _():
        for n in range(4):
            v = r_ref[n, 1, :, 7].astype(F32)
            r_ref[n, 1, :, 7] = jnp.where((wide >= 192) | (row < 8), v, 0.0).astype(BF16)

    def residual(i, carry):
        even, odd = [], []
        for n in range(4):
            pieces = [[], []]
            for e in range(3):
                def tap(shift, low, high):
                    return jnp.concatenate(
                        [
                            r_ref[n, shift, pl.ds(e, 8), i * NI + k, :, low:high].reshape(128, high - low)
                            for k in range(NI)
                        ],
                        axis=0,
                    )

                pieces[0] += [tap(0, 0, 384), tap(1, 128, 384)]
                pieces[1] += [tap(0, 0, 256), tap(1, 0, 384)]
            at = slice(n * 1920, n * 1920 + 1920)
            even.append(dot_nt(jnp.concatenate(pieces[0], axis=1), w0_ref[:, at]))
            odd.append(dot_nt(jnp.concatenate(pieces[1], axis=1), wp_ref[:, at]))
        slot = i & 1
        for parity in range(2):
            if parity == 0:
                p, q = (v[0] + (v[1] + v[2]) for v in (even, odd))
            else:
                p, q = (v[1] - v[2] - v[3] for v in (even, odd))
            p = p.reshape(NI, 8, 2, 8, 192)
            q = q.reshape(NI, 8, 2, 8, 256)
            for k in range(NI):
                for c in range(2):
                    m = (i * NI + k) * 2 + c
                    pk, qk = p[k, :, c], q[k, :, c]
                    now = slice(8 * parity, 8 * parity + 8)
                    left = u_ref[pl.ds(1, 8), m].astype(F32)[:, now]
                    right = u_ref[pl.ds(1, 8), m + 1].astype(F32)[:, now]
                    mid = jnp.where(lane < 64, left[..., 128:256], right[..., 128:256])
                    edge = jnp.concatenate([pk[..., 128:192], jnp.zeros((8, 8, 64), F32)], axis=2)
                    parts = (
                        pk[..., 0:128] + b3[:, 0:128] + left[..., 0:128],
                        edge + qk[..., 0:128] + b3[:, 128:256] + mid,
                        qk[..., 128:256] + b3[:, 256:384] + right[..., 256:384],
                    )
                    for z, part in enumerate(parts):
                        fin_ref[slot, 2 * k + c, parity, z] = part.reshape(64, 128)
        finish(i - 1, 1 - slot)
        return carry

    def finish(i, slot):
        i = jnp.maximum(i, 0)
        for k in range(2 * NI):
            for c in range(3):
                for f in range(16):
                    rows = fin_ref[slot, k, f & 1, c, pl.ds(f >> 1, 8, stride=8), :]
                    at = pl.multiple_of((i * 2 * NI + k) * 384 + c * 128, 128)
                    out_ref[f, :, pl.ds(at, 128)] = rows.astype(BF16)

    wp_ref[0:64, :] = jnp.zeros((64, 7680), BF16)
    w0_copy.wait()
    wp_copy.wait()
    lax.fori_loop(0, 8 // NI, residual, 0)
    finish(8 // NI - 1, (8 // NI - 1) & 1)


def prepare_kernel(
    win_hbm, wup_hbm, wres_hbm, bin_hbm, gin_hbm, bup_hbm, gres_hbm, bres_hbm,
    w1_ref, wc_hbm, w0_hbm, wp_hbm, vec_ref,
    win_ref, wup_ref, wres_ref, bin_ref, gin_ref, bup_ref, gres_ref, bres_ref,
    wc_ref, w0_ref, wp_ref, sems, out_sems,
):
    pairs = (
        (wup_hbm, wup_ref), (wres_hbm, wres_ref), (win_hbm, win_ref), (bin_hbm, bin_ref),
        (gin_hbm, gin_ref), (bup_hbm, bup_ref), (gres_hbm, gres_ref), (bres_hbm, bres_ref),
    )
    copies = [pltpu.make_async_copy(x, y, sems.at[n]) for n, (x, y) in enumerate(pairs)]
    for copy in copies:
        copy.start()
    copies[0].wait()
    taps = [[[0, 1], [2]], [[0], [1, 2]]]
    for dy in range(2):
        for place, dx in enumerate((1, 0)):
            for r in range(2):
                for c in range(2):
                    total = None
                    for b in taps[dy][r]:
                        for e in taps[dx][c]:
                            at = (b * 3 + e) * 384
                            term = wup_ref[:, at : at + 384].astype(F32)
                            total = term if total is None else total + term
                    at = (r * 2 + c) * 384
                    to = (dy * 2 + place) * 192
                    wc_ref[to : to + 192, at : at + 384] = total.astype(BF16)

    wc_copy = pltpu.make_async_copy(wc_ref, wc_hbm, out_sems.at[0])
    wc_copy.start()
    copies[1].wait()
    zero = jnp.zeros((192, 64), BF16)
    for row in range(3):
        g = [wres_ref[:, (time * 3 + row) * 576 : (time * 3 + row) * 576 + 576] for time in range(3)]
        ends = (g[0].astype(F32) + g[2].astype(F32)) * 0.5
        mid = g[1].astype(F32) * 0.5
        taps = (g[0], (ends + mid).astype(BF16), (ends - mid).astype(BF16), g[2])
        for n, tap in enumerate(taps):
            w = [tap[:, e * 192 : e * 192 + 192] for e in range(3)]
            at = slice(n * 1920 + row * 640, n * 1920 + row * 640 + 640)
            w0_ref[:, at] = jnp.concatenate([w[1], w[0], zero, w[2]], axis=1)
            wp_ref[:, at] = jnp.concatenate([w[0], zero, w[2], w[1]], axis=1)
    w0_copy = pltpu.make_async_copy(w0_ref, w0_hbm, out_sems.at[1])
    wp_copy = pltpu.make_async_copy(wp_ref, wp_hbm, out_sems.at[2])
    w0_copy.start()
    wp_copy.start()

    for copy in copies[2:]:
        copy.wait()
    for row in range(3):
        for time in range(3):
            at = row * 256 + time * 64
            w1_ref[at : at + 48] = win_ref[(time * 3 + row) * 48 : (time * 3 + row) * 48 + 48]
            w1_ref[at + 48 : at + 64] = jnp.zeros((16, 384), BF16)
        w1_ref[row * 256 + 192 : row * 256 + 256] = jnp.zeros((64, 384), BF16)

    vec_ref[...] = jnp.zeros((8, 384), F32)
    for row, ref in enumerate((bin_ref, gin_ref)):
        vec_ref[row : row + 1, :] = ref[...].reshape(1, 384)
    for row, ref in enumerate((bup_ref, gres_ref, bres_ref)):
        v = ref[...].reshape(1, 192)
        vec_ref[row + 2 : row + 3, :] = jnp.concatenate([v, v], axis=1)
    wc_copy.wait()
    w0_copy.wait()
    wp_copy.wait()


VMEM_SPEC = pl.BlockSpec(memory_space=pltpu.VMEM)
ANY_SPEC = pl.BlockSpec(memory_space=pl.ANY)
HBM_SPEC = pl.BlockSpec(memory_space=pltpu.HBM)


def local(latents, grid_slot, w_in, b_in, gain_in, w_up, b_up, gain_res, w_res, b_res):
    outbox = pl.pallas_call(
        outbox_kernel,
        out_shape=jax.ShapeDtypeStruct((1024, 128), BF16),
        in_specs=[VMEM_SPEC] * 2,
        out_specs=VMEM_SPEC,
        name="outbox",
    )(grid_slot.reshape(1, 128), latents)
    inbox = lax.all_to_all(
        outbox.reshape(128, 8, 128), ("seq", "tile"), split_axis=0, concat_axis=0, tiled=True
    )
    prepared = pl.pallas_call(
        prepare_kernel,
        out_shape=[
            jax.ShapeDtypeStruct((768, 384), BF16),
            pltpu.HBM((768, 1536), BF16),
            pltpu.HBM((192, 7680), BF16),
            pltpu.HBM((192, 7680), BF16),
            jax.ShapeDtypeStruct((8, 384), F32),
        ],
        in_specs=[HBM_SPEC] * 8,
        out_specs=[VMEM_SPEC] + [HBM_SPEC] * 3 + [VMEM_SPEC],
        scratch_shapes=[
            pltpu.VMEM((432, 384), BF16),
            pltpu.VMEM((192, 3456), BF16),
            pltpu.VMEM((192, 5184), BF16),
            pltpu.VMEM((384,), F32),
            pltpu.VMEM((384,), F32),
            pltpu.VMEM((192,), F32),
            pltpu.VMEM((192,), F32),
            pltpu.VMEM((192,), F32),
            pltpu.VMEM((768, 1536), BF16),
            pltpu.VMEM((192, 7680), BF16),
            pltpu.VMEM((192, 7680), BF16),
            pltpu.SemaphoreType.DMA((8,)),
            pltpu.SemaphoreType.DMA((3,)),
        ],
        cost_estimate=pl.CostEstimate(flops=10_000_000, bytes_accessed=16_000_000, transcendentals=0),
        compiler_params=pltpu.CompilerParams(vmem_limit_bytes=28 * 1024 * 1024),
        name="prepare",
    )(
        *(
            pltpu.with_memory_space_constraint(w, pltpu.HBM)
            for w in (w_in, w_up.T, w_res.T, b_in, gain_in, b_up, gain_res, b_res)
        )
    )
    routed = pl.pallas_call(
        route_kernel,
        out_shape=jax.ShapeDtypeStruct((512, 128), BF16),
        in_specs=[VMEM_SPEC, ANY_SPEC],
        out_specs=VMEM_SPEC,
        compiler_params=pltpu.CompilerParams(vmem_limit_bytes=12 * 1024 * 1024),
        name="route",
    )(inbox.reshape(1024, 128), prepared[4])
    recv = lax.all_to_all(
        routed.reshape(8, 64, 128), "seq", split_axis=0, concat_axis=0, tiled=True
    ).reshape(512, 128)
    return decode(recv, *prepared)


def decode(recv, w1, wc, w0, wp, vec):
    return pl.pallas_call(
        decode_kernel,
        out_shape=jax.ShapeDtypeStruct((16, 8, 6144), BF16),
        in_specs=[VMEM_SPEC] * 2 + [HBM_SPEC] * 3 + [VMEM_SPEC],
        out_specs=VMEM_SPEC,
        scratch_shapes=[
            pltpu.VMEM((3, 8, 4, 16, 128), F32),
            pltpu.VMEM((8, 18, 16, 256), BF16),
            pltpu.VMEM((6, 18, 16, 384), BF16),
            pltpu.VMEM((10, 17, 16, 384), BF16),
            pltpu.VMEM((4, 2, 10, 8, 16, 384), BF16),
            pltpu.VMEM((2, 2 * NI, 2, 3, 64, 128), F32),
            pltpu.VMEM((768, 1536), BF16),
            pltpu.VMEM((192, 7680), BF16),
            pltpu.VMEM((256, 7680), BF16),
            pltpu.SemaphoreType.DMA((3,)),
        ],
        compiler_params=pltpu.CompilerParams(vmem_limit_bytes=44 * 1024 * 1024),
        name="decode",
    )(recv, w1, *(pltpu.with_memory_space_constraint(w, pltpu.HBM) for w in (wc, w0, wp)), vec)


def solution(mesh):
    return jax.shard_map(
        local,
        mesh=mesh,
        in_specs=(P(("seq", "tile"), None), P(("seq", "tile"))) + (P(),) * 8,
        out_specs=P(None, "tile", "seq"),
        check_vma=False,
    )
```

```python
import jax
import jax.numpy as jnp
from jax import lax
from jax.experimental import pallas as pl
from jax.experimental.pallas import tpu as pltpu
from jax.sharding import PartitionSpec as P

F32 = jnp.float32
BF16 = jnp.bfloat16
I32 = jnp.int32
NI = 8


def iota(shape, dim):
    return lax.broadcasted_iota(I32, shape, dim)


def ones_where(cond):
    return jnp.where(cond, 1.0, 0.0).astype(BF16)


def outbox_kernel(slot_ref, lat_ref, out_ref):
    n = 128
    row = jnp.broadcast_to(slot_ref[...], (n, n))
    col = jnp.transpose(row)
    i, j = iota((n, n), 0), iota((n, n), 1)
    same = (row >> 7) == (col >> 7)
    rank_row = jnp.sum(jnp.where(same & (i < j), 1, 0), axis=0, keepdims=True)
    rank_col = jnp.sum(jnp.where(same & (j < i), 1, 0), axis=1, keepdims=True)

    def keys(slot, rank):
        target = slot >> 7
        band = target & 15
        frame, high, group = (slot >> 6) & 1, (slot >> 4) & 3, slot & 15
        upper = high < 2
        halo_target = jnp.where(upper, target - 1, target + 1)
        inside = (upper & (band > 0)) | ((high >= 2) & (band < 15))
        halo_target = jnp.where(inside, halo_target, -1000)
        halo_slot = jnp.where(upper, 4, 2) + rank
        own_label = (frame * 8 + high + 2) * 16 + group + 1
        halo_label = (frame * 8 + jnp.where(upper, high + 6, high - 2)) * 16 + group + 1
        return target, halo_target, halo_slot, own_label, halo_label

    target, halo_target, halo_slot, _, _ = keys(slot_ref[...], rank_row)
    _, _, halo_slot_col, own_label, halo_label = keys(col, rank_col)
    own_table = jnp.where(j == rank_col, own_label, 0).astype(F32).astype(BF16)
    halo_table = jnp.where(j == halo_slot_col, halo_label, 0).astype(F32).astype(BF16)

    q = iota((8 * n, n), 0)
    pick = ones_where((q == target * 8 + rank_row) | (q == halo_target * 8 + halo_slot))
    pick_own = ones_where(q == target * 8 + 6)
    pick_halo = ones_where(q == halo_target * 8 + 6)
    out = jnp.dot(pick, lat_ref[...], preferred_element_type=F32)
    out += jnp.dot(pick_own, own_table, preferred_element_type=F32)
    out += jnp.dot(pick_halo, halo_table, preferred_element_type=F32)
    out_ref[...] = out.astype(BF16)


def route_kernel(inbox_ref, after_ref, out_ref):
    rows = inbox_ref.shape[0]
    inbox = inbox_ref[...]
    boxes = inbox.astype(F32).reshape(rows // 8, 8, 128)
    labels = jnp.broadcast_to(boxes[:, 6:7, :], boxes.shape)
    slot, lane = iota(boxes.shape, 1), iota(boxes.shape, 2)
    label = jnp.sum(jnp.where((slot == lane) & (slot < 6), labels, 0.0), axis=2, keepdims=True)
    label = label.reshape(rows, 1).astype(I32)
    k = iota((1, 512), 1)
    group = 2 * (k >> 6) - 1 + ((k >> 1) & 3)
    wanted = ((k & 1) * 8 + ((k >> 3) & 7)) * 16 + group + 1
    wanted = jnp.where((group >= 0) & (group < 16), wanted, -1)
    pick = ones_where(label == wanted)
    out = lax.dot_general(pick, inbox, (((0,), (0,)), ((), ())), preferred_element_type=F32)
    out_ref[...] = out.astype(BF16)


def dot_nt(x, w):
    return lax.dot_general(x, w, (((1,), (1,)), ((), ())), preferred_element_type=F32)


def silu(v):
    half = 0.5 * v
    return half * jnp.tanh(half) + half


def decode_kernel(
    recv_ref, w1_ref, wc_hbm, w0_hbm, wp_hbm, vec_ref, out_ref,
    grid_ref, x_ref, a_ref, u_ref, r_ref, fin_ref, wc_ref, w0_ref, wp_ref, sems,
):
    s = lax.axis_index("seq")
    t = lax.axis_index("tile")
    wc_copy = pltpu.make_async_copy(wc_hbm, wc_ref, sems.at[0])
    w0_copy = pltpu.make_async_copy(w0_hbm, w0_ref, sems.at[1])
    wp_copy = pltpu.make_async_copy(wp_hbm, wp_ref.at[pl.ds(64, 192)], sems.at[2])
    wc_copy.start()
    w0_copy.start()
    wp_copy.start()
    b1, g1, bc, g2, b3 = (vec_ref[n : n + 1, :] for n in range(5))
    lane = iota((1, 128), 1)

    i, k = iota((512, 128), 0), iota((1, 512), 1)
    key_i = (i >> 4) * 32 + 2 * (i & 7) + ((i >> 3) & 1)
    key_k = ((k >> 1) & 31) * 32 + 2 * (k >> 6) + (k & 1)
    pick = [ones_where(key_i == key_k[:, 128 * n : 128 * n + 128]) for n in range(4)]
    grid_ref[...] = jnp.dot(
        jnp.concatenate(pick, axis=1), recv_ref[...], preferred_element_type=F32
    ).reshape(8, 4, 16, 128)

    def windows(y, carry):
        later = iota((8, 128), 0) > 0
        tiles = [[], [], []]
        for c in range(4):
            now = grid_ref[y, c]
            even, odd = now[0:8], now[8:16]
            even_before = jnp.where(later, pltpu.roll(even, 1, 0), 0.0)
            odd_before = jnp.where(later, pltpu.roll(odd, 1, 0), 0.0)
            tiles[0].append(jnp.concatenate([even_before, odd_before], axis=0))
            tiles[1].append(jnp.concatenate([odd_before, even], axis=0))
            tiles[2].append(now)
        for ix in range(18):
            c, o = divmod((ix + 6) * 16, 128)

            def window(d, to):
                tile = tiles[d][c]
                if o + 48 > 128:
                    tile = jnp.where(lane >= o, tile, tiles[d][c + 1])
                shift = (to - o) % 128
                return pltpu.roll(tile, shift, 1) if shift else tile

            x_ref[y, ix, :, 0:128] = jnp.where(lane < 64, window(0, 0), window(1, 64)).astype(BF16)
            x_ref[y, ix, :, 128:256] = window(2, 0).astype(BF16)
        return carry

    lax.fori_loop(0, 8, windows, 0)

    def first(iy, carry):
        lhs = jnp.concatenate([x_ref[iy + d].reshape(288, 256) for d in range(3)], axis=1)
        v = jnp.dot(lhs, w1_ref[...], preferred_element_type=F32) + b1
        scale = lax.rsqrt(jnp.mean(v * v, axis=1, keepdims=True) + 1e-06)
        a_ref[iy] = silu(v * scale * g1).astype(BF16).reshape(18, 16, 384)
        return carry

    lax.fori_loop(0, 6, first, 0, unroll=True)

    @pl.when(t == 0)
    def _():
        a_ref[0] = jnp.zeros((18, 16, 384), BF16)

    @pl.when(t == lax.axis_size("tile") - 1)
    def _():
        a_ref[5] = jnp.zeros((18, 16, 384), BF16)

    @pl.when(s == 0)
    def _():
        a_ref[:, 0] = jnp.zeros((6, 16, 384), BF16)

    @pl.when(s == lax.axis_size("seq") - 1)
    def _():
        a_ref[:, 17] = jnp.zeros((6, 16, 384), BF16)


    wc_copy.wait()

    def corners(ci, carry):
        lhs = jnp.concatenate(
            [a_ref[ci + d, pl.ds(e, 17)].reshape(272, 384) for d in range(2) for e in range(2)],
            axis=1,
        )
        acc = dot_nt(lhs, wc_ref[...])
        for d in range(2):
            u = (acc[:, 384 * d : 384 * d + 384] + bc).astype(BF16)
            u_ref[2 * ci + d] = u.reshape(17, 16, 384)
            u = u.astype(F32)
            sq = u * u
            mid = sq[:, 128:256]
            low = jnp.sum(sq[:, 0:128] + jnp.where(lane < 64, mid, 0.0), axis=1, keepdims=True)
            top = jnp.sum(sq[:, 256:384] + jnp.where(lane < 64, 0.0, mid), axis=1, keepdims=True)
            low = lax.rsqrt(low * (1 / 192) + 1e-06)
            top = lax.rsqrt(top * (1 / 192) + 1e-06)
            low = jnp.broadcast_to(low, (272, 128))
            top = jnp.broadcast_to(top, (272, 128))
            scale = jnp.concatenate([low, jnp.where(lane < 64, low, top), top], axis=1)
            r = silu(u * scale * g2).reshape(17, 16, 384)
            d2, d3 = r[:, 0:8], r[:, 8:16]
            later = iota((1, 8, 384), 1) > 0
            d0 = jnp.where(later, pltpu.roll(d2, 1, 1), 0.0)
            d1 = jnp.where(later, pltpu.roll(d3, 1, 1), 0.0)
            for n, v in enumerate((d0 - d2, d1 + d2, d2 - d1, d1 - d3)):
                r_ref[n, 0, 2 * ci + d] = v[0:16].reshape(8, 16, 384).astype(BF16)
                r_ref[n, 1, 2 * ci + d] = v[1:17].reshape(8, 16, 384).astype(BF16)
        return carry

    lax.fori_loop(0, 5, corners, 0, unroll=True)

    @pl.when(t == 0)
    def _():
        for n in range(4):
            r_ref[n, :, 0] = jnp.zeros((2, 8, 16, 384), BF16)

    @pl.when(t == lax.axis_size("tile") - 1)
    def _():
        for n in range(4):
            r_ref[n, :, 9] = jnp.zeros((2, 8, 16, 384), BF16)

    row, wide = iota((1, 16, 384), 1), iota((1, 16, 384), 2)

    @pl.when(s == 0)
    def _():
        for n in range(4):
            v = r_ref[n, 0, :, 0].astype(F32)
            r_ref[n, 0, :, 0] = jnp.where((wide < 192) | (row >= 8), v, 0.0).astype(BF16)

    @pl.when(s == lax.axis_size("seq") - 1)
    def _():
        for n in range(4):
            v = r_ref[n, 1, :, 7].astype(F32)
            r_ref[n, 1, :, 7] = jnp.where((wide >= 192) | (row < 8), v, 0.0).astype(BF16)

    def residual(i, carry):
        even, odd = [], []
        for n in range(4):
            def tap(shift, e, low, high):
                return jnp.concatenate(
                    [
                        r_ref[n, shift, pl.ds(e, 8), i * NI + k, :, low:high].reshape(128, high - low)
                        for k in range(NI)
                    ],
                    axis=0,
                )

            def swapped(x):
                return pltpu.roll(x.astype(F32), 64, 1)

            mids = [[tap(shift, e, 128, 256) for e in range(3)] for shift in range(2)]
            left_mid = jnp.where(lane < 64, mids[0][0].astype(F32), swapped(mids[0][1])).astype(BF16)
            right_mid = jnp.where(lane < 64, swapped(mids[1][1]), mids[1][0].astype(F32)).astype(BF16)
            rights = [tap(1, e, 256, 384) for e in range(3)] + [right_mid, mids[1][2]]
            lefts = [tap(0, e, 0, 128) for e in range(3)] + [left_mid, mids[0][2]]
            at = slice(n * 1792, n * 1792 + 1792)
            even_lhs = jnp.concatenate([tap(0, e, 0, 384) for e in range(3)] + rights, axis=1)
            odd_lhs = jnp.concatenate([tap(1, e, 0, 384) for e in range(3)] + lefts, axis=1)
            even.append(dot_nt(even_lhs, w0_ref[:, at]))
            odd.append(dot_nt(odd_lhs, wp_ref[:, at]))
        slot = i & 1
        for parity in range(2):
            if parity == 0:
                p, q = (v[0] + (v[1] + v[2]) for v in (even, odd))
            else:
                p, q = (v[1] - v[2] - v[3] for v in (even, odd))
            p = p.reshape(NI, 8, 2, 8, 192)
            q = q.reshape(NI, 8, 2, 8, 256)
            for k in range(NI):
                for c in range(2):
                    m = (i * NI + k) * 2 + c
                    pk, qk = p[k, :, c], q[k, :, c]
                    now = slice(8 * parity, 8 * parity + 8)
                    left = u_ref[pl.ds(1, 8), m].astype(F32)[:, now]
                    right = u_ref[pl.ds(1, 8), m + 1].astype(F32)[:, now]
                    mid = jnp.where(lane < 64, left[..., 128:256], right[..., 128:256])
                    edge = jnp.concatenate([pk[..., 128:192], jnp.zeros((8, 8, 64), F32)], axis=2)
                    parts = (
                        pk[..., 0:128] + b3[:, 0:128] + left[..., 0:128],
                        edge + qk[..., 0:128] + b3[:, 128:256] + mid,
                        qk[..., 128:256] + b3[:, 256:384] + right[..., 256:384],
                    )
                    for z, part in enumerate(parts):
                        fin_ref[slot, 2 * k + c, parity, z] = part.reshape(64, 128)
        finish(i - 1, 1 - slot)
        return carry

    def finish(i, slot):
        i = jnp.maximum(i, 0)
        for k in range(2 * NI):
            for c in range(3):
                for f in range(16):
                    rows = fin_ref[slot, k, f & 1, c, pl.ds(f >> 1, 8, stride=8), :]
                    at = pl.multiple_of((i * 2 * NI + k) * 384 + c * 128, 128)
                    out_ref[f, :, pl.ds(at, 128)] = rows.astype(BF16)

    wp_ref[0:64, :] = jnp.zeros((64, 7168), BF16)
    w0_copy.wait()
    wp_copy.wait()
    lax.fori_loop(0, 8 // NI, residual, 0)
    finish(8 // NI - 1, (8 // NI - 1) & 1)


def prepare_kernel(
    win_hbm, wup_hbm, wres_hbm, bin_hbm, gin_hbm, bup_hbm, gres_hbm, bres_hbm,
    w1_ref, wc_hbm, w0_hbm, wp_hbm, vec_ref,
    win_ref, wup_ref, wres_ref, bin_ref, gin_ref, bup_ref, gres_ref, bres_ref,
    wc_ref, w0_ref, wp_ref, sems, in_sems, out_sems,
):
    chunks = [pl.ds(48 * n, 48) for n in range(4)]
    res_in = [
        pltpu.make_async_copy(wres_hbm.at[at], wres_ref.at[at], in_sems.at[0, n])
        for n, at in enumerate(chunks)
    ]
    up_in = [
        pltpu.make_async_copy(wup_hbm.at[at], wup_ref.at[at], in_sems.at[1, n])
        for n, at in enumerate(chunks)
    ]
    pairs = (
        (win_hbm, win_ref), (bin_hbm, bin_ref), (gin_hbm, gin_ref), (bup_hbm, bup_ref),
        (gres_hbm, gres_ref), (bres_hbm, bres_ref),
    )
    rest = [pltpu.make_async_copy(x, y, sems.at[n]) for n, (x, y) in enumerate(pairs)]
    for copy in res_in + up_in + rest:
        copy.start()

    outs = []
    zero = jnp.zeros((48, 64), BF16)
    for chunk, rows in enumerate(chunks):
        res_in[chunk].wait()
        kinds = [[], [], [], []]
        for row in range(3):
            g = [wres_ref[rows, (time * 3 + row) * 576 : (time * 3 + row) * 576 + 576] for time in range(3)]
            ends = (g[0].astype(F32) + g[2].astype(F32)) * 0.5
            mid = g[1].astype(F32) * 0.5
            for kind, tap in zip(kinds, (g[0], (ends + mid).astype(BF16), (ends - mid).astype(BF16), g[2])):
                kind.append([tap[:, e * 192 : e * 192 + 192] for e in range(3)])
        for n, w in enumerate(kinds):
            at = slice(n * 1792, n * 1792 + 1792)
            even = [w[e][x] for e in range(3) for x in (1, 0)]
            even += [w[e][2][:, 64:192] for e in range(3)]
            even += [w[1][2][:, 0:64], w[0][2][:, 0:64], zero, w[2][2][:, 0:64]]
            odd = [w[e][x] for e in range(3) for x in (2, 1)]
            odd += [w[e][0][:, 0:128] for e in range(3)]
            odd += [w[0][0][:, 128:192], w[1][0][:, 128:192], w[2][0][:, 128:192], zero]
            w0_ref[rows, at] = jnp.concatenate(even, axis=1)
            wp_ref[rows, at] = jnp.concatenate(odd, axis=1)
        outs.append(pltpu.make_async_copy(w0_ref.at[rows], w0_hbm.at[rows], out_sems.at[0, chunk]))
        outs.append(pltpu.make_async_copy(wp_ref.at[rows], wp_hbm.at[rows], out_sems.at[1, chunk]))
        outs[-2].start()
        outs[-1].start()

    taps = [[[0, 1], [2]], [[0], [1, 2]]]
    for copy in up_in:
        copy.wait()
    for dy in range(2):
        for place, dx in enumerate((1, 0)):
            to = (dy * 2 + place) * 192
            for r in range(2):
                for c in range(2):
                    total = None
                    for b in taps[dy][r]:
                        for e in taps[dx][c]:
                            at = (b * 3 + e) * 384
                            term = wup_ref[:, at : at + 384].astype(F32)
                            total = term if total is None else total + term
                    at = (r * 2 + c) * 384
                    wc_ref[to : to + 192, at : at + 384] = total.astype(BF16)
            rows = pl.ds(to, 192)
            outs.append(pltpu.make_async_copy(wc_ref.at[rows], wc_hbm.at[rows], out_sems.at[2, dy * 2 + place]))
            outs[-1].start()

    for copy in rest:
        copy.wait()
    for row in range(3):
        for time in range(3):
            at = row * 256 + time * 64
            w1_ref[at : at + 48] = win_ref[(time * 3 + row) * 48 : (time * 3 + row) * 48 + 48]
            w1_ref[at + 48 : at + 64] = jnp.zeros((16, 384), BF16)
        w1_ref[row * 256 + 192 : row * 256 + 256] = jnp.zeros((64, 384), BF16)

    vec_ref[...] = jnp.zeros((8, 384), F32)
    for row, ref in enumerate((bin_ref, gin_ref)):
        vec_ref[row : row + 1, :] = ref[...].reshape(1, 384)
    for row, ref in enumerate((bup_ref, gres_ref, bres_ref)):
        v = ref[...].reshape(1, 192)
        vec_ref[row + 2 : row + 3, :] = jnp.concatenate([v, v], axis=1)
    for copy in outs:
        copy.wait()


VMEM_SPEC = pl.BlockSpec(memory_space=pltpu.VMEM)
ANY_SPEC = pl.BlockSpec(memory_space=pl.ANY)
HBM_SPEC = pl.BlockSpec(memory_space=pltpu.HBM)


def local(latents, grid_slot, w_in, b_in, gain_in, w_up, b_up, gain_res, w_res, b_res):
    outbox = pl.pallas_call(
        outbox_kernel,
        out_shape=jax.ShapeDtypeStruct((1024, 128), BF16),
        in_specs=[VMEM_SPEC] * 2,
        out_specs=VMEM_SPEC,
        name="outbox",
    )(grid_slot.reshape(1, 128), latents)
    inbox = lax.all_to_all(
        outbox.reshape(128, 8, 128), ("seq", "tile"), split_axis=0, concat_axis=0, tiled=True
    )
    prepared = pl.pallas_call(
        prepare_kernel,
        out_shape=[
            jax.ShapeDtypeStruct((768, 384), BF16),
            pltpu.HBM((768, 1536), BF16),
            pltpu.HBM((192, 7168), BF16),
            pltpu.HBM((192, 7168), BF16),
            jax.ShapeDtypeStruct((8, 384), F32),
        ],
        in_specs=[HBM_SPEC] * 8,
        out_specs=[VMEM_SPEC] + [HBM_SPEC] * 3 + [VMEM_SPEC],
        scratch_shapes=[
            pltpu.VMEM((432, 384), BF16),
            pltpu.VMEM((192, 3456), BF16),
            pltpu.VMEM((192, 5184), BF16),
            pltpu.VMEM((384,), F32),
            pltpu.VMEM((384,), F32),
            pltpu.VMEM((192,), F32),
            pltpu.VMEM((192,), F32),
            pltpu.VMEM((192,), F32),
            pltpu.VMEM((768, 1536), BF16),
            pltpu.VMEM((192, 7168), BF16),
            pltpu.VMEM((192, 7168), BF16),
            pltpu.SemaphoreType.DMA((6,)),
            pltpu.SemaphoreType.DMA((2, 4)),
            pltpu.SemaphoreType.DMA((3, 4)),
        ],
        cost_estimate=pl.CostEstimate(flops=10_000_000, bytes_accessed=16_000_000, transcendentals=0),
        compiler_params=pltpu.CompilerParams(vmem_limit_bytes=28 * 1024 * 1024),
        name="prepare",
    )(
        *(
            pltpu.with_memory_space_constraint(w, pltpu.HBM)
            for w in (w_in, w_up.T, w_res.T, b_in, gain_in, b_up, gain_res, b_res)
        )
    )
    routed = pl.pallas_call(
        route_kernel,
        out_shape=jax.ShapeDtypeStruct((512, 128), BF16),
        in_specs=[VMEM_SPEC, ANY_SPEC],
        out_specs=VMEM_SPEC,
        compiler_params=pltpu.CompilerParams(vmem_limit_bytes=12 * 1024 * 1024),
        name="route",
    )(inbox.reshape(1024, 128), prepared[4])
    recv = lax.all_to_all(
        routed.reshape(8, 64, 128), "seq", split_axis=0, concat_axis=0, tiled=True
    ).reshape(512, 128)
    return decode(recv, *prepared)


def decode(recv, w1, wc, w0, wp, vec):
    return pl.pallas_call(
        decode_kernel,
        out_shape=jax.ShapeDtypeStruct((16, 8, 6144), BF16),
        in_specs=[VMEM_SPEC] * 2 + [HBM_SPEC] * 3 + [VMEM_SPEC],
        out_specs=VMEM_SPEC,
        scratch_shapes=[
            pltpu.VMEM((8, 4, 16, 128), F32),
            pltpu.VMEM((8, 18, 16, 256), BF16),
            pltpu.VMEM((6, 18, 16, 384), BF16),
            pltpu.VMEM((10, 17, 16, 384), BF16),
            pltpu.VMEM((4, 2, 10, 8, 16, 384), BF16),
            pltpu.VMEM((2, 2 * NI, 2, 3, 64, 128), F32),
            pltpu.VMEM((768, 1536), BF16),
            pltpu.VMEM((192, 7168), BF16),
            pltpu.VMEM((256, 7168), BF16),
            pltpu.SemaphoreType.DMA((3,)),
        ],
        compiler_params=pltpu.CompilerParams(vmem_limit_bytes=44 * 1024 * 1024),
        name="decode",
    )(recv, w1, *(pltpu.with_memory_space_constraint(w, pltpu.HBM) for w in (wc, w0, wp)), vec)


def solution(mesh):
    return jax.shard_map(
        local,
        mesh=mesh,
        in_specs=(P(("seq", "tile"), None), P(("seq", "tile"))) + (P(),) * 8,
        out_specs=P(None, "tile", "seq"),
        check_vma=False,
    )
```

```python
import jax
import jax.numpy as jnp
from jax import lax
from jax.experimental import pallas as pl
from jax.experimental.pallas import tpu as pltpu
from jax.sharding import PartitionSpec as P

F32 = jnp.float32
BF16 = jnp.bfloat16
I32 = jnp.int32
NI = 8


def iota(shape, dim):
    return lax.broadcasted_iota(I32, shape, dim)


def ones_where(cond):
    return jnp.where(cond, 1.0, 0.0).astype(BF16)


def outbox_kernel(slot_ref, lat_ref, out_ref):
    n = 128
    row = jnp.broadcast_to(slot_ref[...], (n, n))
    col = jnp.transpose(row)
    i, j = iota((n, n), 0), iota((n, n), 1)
    same = (row >> 7) == (col >> 7)
    rank_row = jnp.sum(jnp.where(same & (i < j), 1, 0), axis=0, keepdims=True)
    rank_col = jnp.sum(jnp.where(same & (j < i), 1, 0), axis=1, keepdims=True)

    def keys(slot, rank):
        target = slot >> 7
        band = target & 15
        frame, high, group = (slot >> 6) & 1, (slot >> 4) & 3, slot & 15
        upper = high < 2
        halo_target = jnp.where(upper, target - 1, target + 1)
        inside = (upper & (band > 0)) | ((high >= 2) & (band < 15))
        halo_target = jnp.where(inside, halo_target, -1000)
        halo_slot = jnp.where(upper, 4, 2) + rank
        own_label = (frame * 8 + high + 2) * 16 + group + 1
        halo_label = (frame * 8 + jnp.where(upper, high + 6, high - 2)) * 16 + group + 1
        return target, halo_target, halo_slot, own_label, halo_label

    target, halo_target, halo_slot, _, _ = keys(slot_ref[...], rank_row)
    _, _, halo_slot_col, own_label, halo_label = keys(col, rank_col)
    own_table = jnp.where(j == rank_col, own_label, 0).astype(F32).astype(BF16)
    halo_table = jnp.where(j == halo_slot_col, halo_label, 0).astype(F32).astype(BF16)

    q = iota((8 * n, n), 0)
    pick = ones_where((q == target * 8 + rank_row) | (q == halo_target * 8 + halo_slot))
    pick_own = ones_where(q == target * 8 + 6)
    pick_halo = ones_where(q == halo_target * 8 + 6)
    out = jnp.dot(pick, lat_ref[...], preferred_element_type=F32)
    out += jnp.dot(pick_own, own_table, preferred_element_type=F32)
    out += jnp.dot(pick_halo, halo_table, preferred_element_type=F32)
    out_ref[...] = out.astype(BF16)


def route_kernel(inbox_ref, after_ref, out_ref):
    rows = inbox_ref.shape[0]
    inbox = inbox_ref[...]
    boxes = inbox.astype(F32).reshape(rows // 8, 8, 128)
    labels = jnp.broadcast_to(boxes[:, 6:7, :], boxes.shape)
    slot, lane = iota(boxes.shape, 1), iota(boxes.shape, 2)
    label = jnp.sum(jnp.where((slot == lane) & (slot < 6), labels, 0.0), axis=2, keepdims=True)
    label = label.reshape(rows, 1).astype(I32)
    k = iota((1, 512), 1)
    group = 2 * (k >> 6) - 1 + ((k >> 1) & 3)
    wanted = ((k & 1) * 8 + ((k >> 3) & 7)) * 16 + group + 1
    wanted = jnp.where((group >= 0) & (group < 16), wanted, -1)
    pick = ones_where(label == wanted)
    out = lax.dot_general(pick, inbox, (((0,), (0,)), ((), ())), preferred_element_type=F32)
    out_ref[...] = out.astype(BF16)


def dot_nt(x, w):
    return lax.dot_general(x, w, (((1,), (1,)), ((), ())), preferred_element_type=F32)


def silu(v):
    half = 0.5 * v
    return half * jnp.tanh(half) + half


def decode_kernel(
    recv_ref, w1_ref, wc_hbm, w0_hbm, wp_hbm, vec_ref, out_ref,
    grid_ref, x_ref, a_ref, u_ref, r_ref, fin_ref, wc_ref, w0_ref, wp_ref, sems,
):
    s = lax.axis_index("seq")
    t = lax.axis_index("tile")
    wc_copy = pltpu.make_async_copy(wc_hbm, wc_ref, sems.at[0])
    w0_copy = pltpu.make_async_copy(w0_hbm, w0_ref, sems.at[1])
    wp_copy = pltpu.make_async_copy(wp_hbm, wp_ref.at[pl.ds(64, 192)], sems.at[2])
    wc_copy.start()
    w0_copy.start()
    wp_copy.start()
    b1, g1, bc, g2, b3 = (vec_ref[n : n + 1, :] for n in range(5))
    lane = iota((1, 128), 1)

    i, k = iota((512, 128), 0), iota((1, 512), 1)
    key_i = (i >> 4) * 32 + 2 * (i & 7) + ((i >> 3) & 1)
    key_k = ((k >> 1) & 31) * 32 + 2 * (k >> 6) + (k & 1)
    pick = [ones_where(key_i == key_k[:, 128 * n : 128 * n + 128]) for n in range(4)]
    grid_ref[...] = jnp.dot(
        jnp.concatenate(pick, axis=1), recv_ref[...], preferred_element_type=F32
    ).reshape(8, 4, 16, 128)

    def windows(y):
        later = iota((8, 128), 0) > 0
        tiles = [[], [], []]
        for c in range(4):
            now = grid_ref[y, c]
            even, odd = now[0:8], now[8:16]
            even_before = jnp.where(later, pltpu.roll(even, 1, 0), 0.0)
            odd_before = jnp.where(later, pltpu.roll(odd, 1, 0), 0.0)
            tiles[0].append(jnp.concatenate([even_before, odd_before], axis=0))
            tiles[1].append(jnp.concatenate([odd_before, even], axis=0))
            tiles[2].append(now)
        for ix in range(18):
            c, o = divmod((ix + 6) * 16, 128)

            def window(d, to):
                tile = tiles[d][c]
                if o + 48 > 128:
                    tile = jnp.where(lane >= o, tile, tiles[d][c + 1])
                shift = (to - o) % 128
                return pltpu.roll(tile, shift, 1) if shift else tile

            x_ref[y, ix, :, 0:128] = jnp.where(lane < 64, window(0, 0), window(1, 64)).astype(BF16)
            x_ref[y, ix, :, 128:256] = window(2, 0).astype(BF16)

    for y in range(8):
        windows(y)

    def inside(condition):
        return jnp.where(condition, 1.0, 0.0)

    has_low_row, has_high_row = inside(t > 0), inside(t < lax.axis_size("tile") - 1)
    has_low_col, has_high_col = inside(s > 0), inside(s < lax.axis_size("seq") - 1)

    def first(iy):
        lhs = jnp.concatenate([x_ref[iy + d].reshape(288, 256) for d in range(3)], axis=1)
        v = jnp.dot(lhs, w1_ref[...], preferred_element_type=F32) + b1
        scale = lax.rsqrt(jnp.mean(v * v, axis=1, keepdims=True) + 1e-06)
        row = iota((288, 1), 0)
        scale = jnp.where(row < 16, scale * has_low_col, scale)
        scale = jnp.where(row >= 272, scale * has_high_col, scale)
        if iy == 0:
            scale = scale * has_low_row
        if iy == 5:
            scale = scale * has_high_row
        a_ref[iy] = silu(v * scale * g1).astype(BF16).reshape(18, 16, 384)

    for iy in range(6):
        first(iy)

    wc_copy.wait()

    def corners(ci):
        lhs = jnp.concatenate(
            [a_ref[ci + d, e : e + 17].reshape(272, 384) for d in range(2) for e in range(2)],
            axis=1,
        )
        acc = dot_nt(lhs, wc_ref[...])
        for d in range(2):
            u = (acc[:, 384 * d : 384 * d + 384] + bc).astype(BF16)
            u_ref[2 * ci + d] = u.reshape(17, 16, 384)
            u = u.astype(F32)
            sq = u * u
            mid = sq[:, 128:256]
            low = jnp.sum(sq[:, 0:128] + jnp.where(lane < 64, mid, 0.0), axis=1, keepdims=True)
            top = jnp.sum(sq[:, 256:384] + jnp.where(lane < 64, 0.0, mid), axis=1, keepdims=True)
            low = lax.rsqrt(low * (1 / 192) + 1e-06)
            top = lax.rsqrt(top * (1 / 192) + 1e-06)
            row = iota((272, 1), 0)
            low = jnp.where(row >= 256, low * has_high_col, low)
            top = jnp.where(row < 16, top * has_low_col, top)
            if 2 * ci + d == 0:
                low, top = low * has_low_row, top * has_low_row
            if 2 * ci + d == 9:
                low, top = low * has_high_row, top * has_high_row
            low = jnp.broadcast_to(low, (272, 128))
            top = jnp.broadcast_to(top, (272, 128))
            scale = jnp.concatenate([low, jnp.where(lane < 64, low, top), top], axis=1)
            r = silu(u * scale * g2).reshape(17, 16, 384)
            d2, d3 = r[:, 0:8], r[:, 8:16]
            later = iota((1, 8, 384), 1) > 0
            d0 = jnp.where(later, pltpu.roll(d2, 1, 1), 0.0)
            d1 = jnp.where(later, pltpu.roll(d3, 1, 1), 0.0)
            for n, v in enumerate((d0 - d2, d1 + d2, d2 - d1, d1 - d3)):
                r_ref[n, 0, 2 * ci + d] = v[0:16].reshape(8, 16, 384).astype(BF16)
                r_ref[n, 1, 2 * ci + d] = v[1:17].reshape(8, 16, 384).astype(BF16)

    for ci in range(5):
        corners(ci)

    def residual(i, carry):
        even, odd = [], []
        for n in range(4):
            def tap(shift, e, low, high):
                return jnp.concatenate(
                    [
                        r_ref[n, shift, pl.ds(e, 8), i * NI + k, :, low:high].reshape(128, high - low)
                        for k in range(NI)
                    ],
                    axis=0,
                )

            def swapped(x):
                return pltpu.roll(x.astype(F32), 64, 1)

            mids = [[tap(shift, e, 128, 256) for e in range(3)] for shift in range(2)]
            left_mid = jnp.where(lane < 64, mids[0][0].astype(F32), swapped(mids[0][1])).astype(BF16)
            right_mid = jnp.where(lane < 64, swapped(mids[1][1]), mids[1][0].astype(F32)).astype(BF16)
            rights = [tap(1, e, 256, 384) for e in range(3)] + [right_mid, mids[1][2]]
            lefts = [tap(0, e, 0, 128) for e in range(3)] + [left_mid, mids[0][2]]
            at = slice(n * 1792, n * 1792 + 1792)
            even_lhs = jnp.concatenate([tap(0, e, 0, 384) for e in range(3)] + rights, axis=1)
            odd_lhs = jnp.concatenate([tap(1, e, 0, 384) for e in range(3)] + lefts, axis=1)
            even.append(dot_nt(even_lhs, w0_ref[:, at]))
            odd.append(dot_nt(odd_lhs, wp_ref[:, at]))
        slot = i & 1
        for parity in range(2):
            if parity == 0:
                p, q = (v[0] + (v[1] + v[2]) for v in (even, odd))
            else:
                p, q = (v[1] - v[2] - v[3] for v in (even, odd))
            p = p.reshape(NI, 8, 2, 8, 192)
            q = q.reshape(NI, 8, 2, 8, 256)
            for k in range(NI):
                for c in range(2):
                    m = (i * NI + k) * 2 + c
                    pk, qk = p[k, :, c], q[k, :, c]
                    now = slice(8 * parity, 8 * parity + 8)
                    left = u_ref[pl.ds(1, 8), m].astype(F32)[:, now]
                    right = u_ref[pl.ds(1, 8), m + 1].astype(F32)[:, now]
                    mid = jnp.where(lane < 64, left[..., 128:256], right[..., 128:256])
                    edge = jnp.concatenate([pk[..., 128:192], jnp.zeros((8, 8, 64), F32)], axis=2)
                    parts = (
                        pk[..., 0:128] + b3[:, 0:128] + left[..., 0:128],
                        edge + qk[..., 0:128] + b3[:, 128:256] + mid,
                        qk[..., 128:256] + b3[:, 256:384] + right[..., 256:384],
                    )
                    for z, part in enumerate(parts):
                        fin_ref[slot, 2 * k + c, parity, z] = part.reshape(64, 128)
        finish(i - 1, 1 - slot)
        return carry

    def finish(i, slot):
        i = jnp.maximum(i, 0)
        for k in range(2 * NI):
            for c in range(3):
                for f in range(16):
                    rows = fin_ref[slot, k, f & 1, c, pl.ds(f >> 1, 8, stride=8), :]
                    at = pl.multiple_of((i * 2 * NI + k) * 384 + c * 128, 128)
                    out_ref[f, :, pl.ds(at, 128)] = rows.astype(BF16)

    wp_ref[0:64, :] = jnp.zeros((64, 7168), BF16)
    w0_copy.wait()
    wp_copy.wait()
    lax.fori_loop(0, 8 // NI, residual, 0)
    finish(8 // NI - 1, (8 // NI - 1) & 1)


def prepare_kernel(
    win_hbm, wup_hbm, wres_hbm, bin_hbm, gin_hbm, bup_hbm, gres_hbm, bres_hbm,
    w1_ref, wc_hbm, w0_hbm, wp_hbm, vec_ref,
    win_ref, wup_ref, wres_ref, bin_ref, gin_ref, bup_ref, gres_ref, bres_ref,
    wc_ref, w0_ref, wp_ref, sems, in_sems, out_sems,
):
    chunks = [pl.ds(48 * n, 48) for n in range(4)]
    res_in = [
        pltpu.make_async_copy(wres_hbm.at[at], wres_ref.at[at], in_sems.at[0, n])
        for n, at in enumerate(chunks)
    ]
    up_in = [
        pltpu.make_async_copy(wup_hbm.at[at], wup_ref.at[at], in_sems.at[1, n])
        for n, at in enumerate(chunks)
    ]
    pairs = (
        (win_hbm, win_ref), (bin_hbm, bin_ref), (gin_hbm, gin_ref), (bup_hbm, bup_ref),
        (gres_hbm, gres_ref), (bres_hbm, bres_ref),
    )
    rest = [pltpu.make_async_copy(x, y, sems.at[n]) for n, (x, y) in enumerate(pairs)]
    for copy in res_in + up_in + rest:
        copy.start()

    outs = []
    zero = jnp.zeros((48, 64), BF16)
    for chunk, rows in enumerate(chunks):
        res_in[chunk].wait()
        kinds = [[], [], [], []]
        for row in range(3):
            g = [wres_ref[rows, (time * 3 + row) * 576 : (time * 3 + row) * 576 + 576] for time in range(3)]
            ends = (g[0].astype(F32) + g[2].astype(F32)) * 0.5
            mid = g[1].astype(F32) * 0.5
            for kind, tap in zip(kinds, (g[0], (ends + mid).astype(BF16), (ends - mid).astype(BF16), g[2])):
                kind.append([tap[:, e * 192 : e * 192 + 192] for e in range(3)])
        for n, w in enumerate(kinds):
            at = slice(n * 1792, n * 1792 + 1792)
            even = [w[e][x] for e in range(3) for x in (1, 0)]
            even += [w[e][2][:, 64:192] for e in range(3)]
            even += [w[1][2][:, 0:64], w[0][2][:, 0:64], zero, w[2][2][:, 0:64]]
            odd = [w[e][x] for e in range(3) for x in (2, 1)]
            odd += [w[e][0][:, 0:128] for e in range(3)]
            odd += [w[0][0][:, 128:192], w[1][0][:, 128:192], w[2][0][:, 128:192], zero]
            w0_ref[rows, at] = jnp.concatenate(even, axis=1)
            wp_ref[rows, at] = jnp.concatenate(odd, axis=1)
        outs.append(pltpu.make_async_copy(w0_ref.at[rows], w0_hbm.at[rows], out_sems.at[0, chunk]))
        outs.append(pltpu.make_async_copy(wp_ref.at[rows], wp_hbm.at[rows], out_sems.at[1, chunk]))
        outs[-2].start()
        outs[-1].start()

    taps = [[[0, 1], [2]], [[0], [1, 2]]]
    for copy in up_in:
        copy.wait()
    for dy in range(2):
        for place, dx in enumerate((1, 0)):
            to = (dy * 2 + place) * 192
            for r in range(2):
                for c in range(2):
                    total = None
                    for b in taps[dy][r]:
                        for e in taps[dx][c]:
                            at = (b * 3 + e) * 384
                            term = wup_ref[:, at : at + 384].astype(F32)
                            total = term if total is None else total + term
                    at = (r * 2 + c) * 384
                    wc_ref[to : to + 192, at : at + 384] = total.astype(BF16)
            rows = pl.ds(to, 192)
            outs.append(pltpu.make_async_copy(wc_ref.at[rows], wc_hbm.at[rows], out_sems.at[2, dy * 2 + place]))
            outs[-1].start()

    for copy in rest:
        copy.wait()
    for row in range(3):
        for time in range(3):
            at = row * 256 + time * 64
            w1_ref[at : at + 48] = win_ref[(time * 3 + row) * 48 : (time * 3 + row) * 48 + 48]
            w1_ref[at + 48 : at + 64] = jnp.zeros((16, 384), BF16)
        w1_ref[row * 256 + 192 : row * 256 + 256] = jnp.zeros((64, 384), BF16)

    vec_ref[...] = jnp.zeros((8, 384), F32)
    for row, ref in enumerate((bin_ref, gin_ref)):
        vec_ref[row : row + 1, :] = ref[...].reshape(1, 384)
    for row, ref in enumerate((bup_ref, gres_ref, bres_ref)):
        v = ref[...].reshape(1, 192)
        vec_ref[row + 2 : row + 3, :] = jnp.concatenate([v, v], axis=1)
    for copy in outs:
        copy.wait()


VMEM_SPEC = pl.BlockSpec(memory_space=pltpu.VMEM)
ANY_SPEC = pl.BlockSpec(memory_space=pl.ANY)
HBM_SPEC = pl.BlockSpec(memory_space=pltpu.HBM)


def local(latents, grid_slot, w_in, b_in, gain_in, w_up, b_up, gain_res, w_res, b_res):
    outbox = pl.pallas_call(
        outbox_kernel,
        out_shape=jax.ShapeDtypeStruct((1024, 128), BF16),
        in_specs=[VMEM_SPEC] * 2,
        out_specs=VMEM_SPEC,
        name="outbox",
    )(grid_slot.reshape(1, 128), latents)
    inbox = lax.all_to_all(
        outbox.reshape(128, 8, 128), ("seq", "tile"), split_axis=0, concat_axis=0, tiled=True
    )
    prepared = pl.pallas_call(
        prepare_kernel,
        out_shape=[
            jax.ShapeDtypeStruct((768, 384), BF16),
            pltpu.HBM((768, 1536), BF16),
            pltpu.HBM((192, 7168), BF16),
            pltpu.HBM((192, 7168), BF16),
            jax.ShapeDtypeStruct((8, 384), F32),
        ],
        in_specs=[HBM_SPEC] * 8,
        out_specs=[VMEM_SPEC] + [HBM_SPEC] * 3 + [VMEM_SPEC],
        scratch_shapes=[
            pltpu.VMEM((432, 384), BF16),
            pltpu.VMEM((192, 3456), BF16),
            pltpu.VMEM((192, 5184), BF16),
            pltpu.VMEM((384,), F32),
            pltpu.VMEM((384,), F32),
            pltpu.VMEM((192,), F32),
            pltpu.VMEM((192,), F32),
            pltpu.VMEM((192,), F32),
            pltpu.VMEM((768, 1536), BF16),
            pltpu.VMEM((192, 7168), BF16),
            pltpu.VMEM((192, 7168), BF16),
            pltpu.SemaphoreType.DMA((6,)),
            pltpu.SemaphoreType.DMA((2, 4)),
            pltpu.SemaphoreType.DMA((3, 4)),
        ],
        cost_estimate=pl.CostEstimate(flops=10_000_000, bytes_accessed=16_000_000, transcendentals=0),
        compiler_params=pltpu.CompilerParams(vmem_limit_bytes=28 * 1024 * 1024),
        name="prepare",
    )(
        *(
            pltpu.with_memory_space_constraint(w, pltpu.HBM)
            for w in (w_in, w_up.T, w_res.T, b_in, gain_in, b_up, gain_res, b_res)
        )
    )
    routed = pl.pallas_call(
        route_kernel,
        out_shape=jax.ShapeDtypeStruct((512, 128), BF16),
        in_specs=[VMEM_SPEC, ANY_SPEC],
        out_specs=VMEM_SPEC,
        compiler_params=pltpu.CompilerParams(vmem_limit_bytes=12 * 1024 * 1024),
        name="route",
    )(inbox.reshape(1024, 128), prepared[4])
    recv = lax.all_to_all(
        routed.reshape(8, 64, 128), "seq", split_axis=0, concat_axis=0, tiled=True
    ).reshape(512, 128)
    return decode(recv, *prepared)


def decode(recv, w1, wc, w0, wp, vec):
    return pl.pallas_call(
        decode_kernel,
        out_shape=jax.ShapeDtypeStruct((16, 8, 6144), BF16),
        in_specs=[VMEM_SPEC] * 2 + [HBM_SPEC] * 3 + [VMEM_SPEC],
        out_specs=VMEM_SPEC,
        scratch_shapes=[
            pltpu.VMEM((8, 4, 16, 128), F32),
            pltpu.VMEM((8, 18, 16, 256), BF16),
            pltpu.VMEM((6, 18, 16, 384), BF16),
            pltpu.VMEM((10, 17, 16, 384), BF16),
            pltpu.VMEM((4, 2, 10, 8, 16, 384), BF16),
            pltpu.VMEM((2, 2 * NI, 2, 3, 64, 128), F32),
            pltpu.VMEM((768, 1536), BF16),
            pltpu.VMEM((192, 7168), BF16),
            pltpu.VMEM((256, 7168), BF16),
            pltpu.SemaphoreType.DMA((3,)),
        ],
        compiler_params=pltpu.CompilerParams(vmem_limit_bytes=44 * 1024 * 1024),
        name="decode",
    )(recv, w1, *(pltpu.with_memory_space_constraint(w, pltpu.HBM) for w in (wc, w0, wp)), vec)


def solution(mesh):
    return jax.shard_map(
        local,
        mesh=mesh,
        in_specs=(P(("seq", "tile"), None), P(("seq", "tile"))) + (P(),) * 8,
        out_specs=P(None, "tile", "seq"),
        check_vma=False,
    )
```

```python
import jax
import jax.numpy as jnp
from jax import lax
from jax.experimental import pallas as pl
from jax.experimental.pallas import tpu as pltpu
from jax.sharding import PartitionSpec as P

F32 = jnp.float32
BF16 = jnp.bfloat16
I32 = jnp.int32
NI = 8


def iota(shape, dim):
    return lax.broadcasted_iota(I32, shape, dim)


def ones_where(cond):
    return jnp.where(cond, 1.0, 0.0).astype(BF16)


def outbox_kernel(slot_ref, lat_ref, out_ref):
    n = 128
    row = jnp.broadcast_to(slot_ref[...], (n, n))
    col = jnp.transpose(row)
    i, j = iota((n, n), 0), iota((n, n), 1)
    same = (row >> 7) == (col >> 7)
    rank_row = jnp.sum(jnp.where(same & (i < j), 1, 0), axis=0, keepdims=True)
    rank_col = jnp.sum(jnp.where(same & (j < i), 1, 0), axis=1, keepdims=True)

    def keys(slot, rank):
        target = slot >> 7
        band = target & 15
        frame, high, group = (slot >> 6) & 1, (slot >> 4) & 3, slot & 15
        upper = high < 2
        halo_target = jnp.where(upper, target - 1, target + 1)
        inside = (upper & (band > 0)) | ((high >= 2) & (band < 15))
        halo_target = jnp.where(inside, halo_target, -1000)
        halo_slot = jnp.where(upper, 4, 2) + rank
        own_label = (frame * 8 + high + 2) * 16 + group + 1
        halo_label = (frame * 8 + jnp.where(upper, high + 6, high - 2)) * 16 + group + 1
        return target, halo_target, halo_slot, own_label, halo_label

    target, halo_target, halo_slot, _, _ = keys(slot_ref[...], rank_row)
    _, _, halo_slot_col, own_label, halo_label = keys(col, rank_col)
    own_table = jnp.where(j == rank_col, own_label, 0).astype(F32).astype(BF16)
    halo_table = jnp.where(j == halo_slot_col, halo_label, 0).astype(F32).astype(BF16)

    q = iota((8 * n, n), 0)
    pick = ones_where((q == target * 8 + rank_row) | (q == halo_target * 8 + halo_slot))
    pick_own = ones_where(q == target * 8 + 6)
    pick_halo = ones_where(q == halo_target * 8 + 6)
    out = jnp.dot(pick, lat_ref[...], preferred_element_type=F32)
    out += jnp.dot(pick_own, own_table, preferred_element_type=F32)
    out += jnp.dot(pick_halo, halo_table, preferred_element_type=F32)
    out_ref[...] = out.astype(BF16)


def route_kernel(inbox_ref, after_ref, out_ref):
    rows = inbox_ref.shape[0]
    inbox = inbox_ref[...]
    boxes = inbox.astype(F32).reshape(rows // 8, 8, 128)
    labels = jnp.broadcast_to(boxes[:, 6:7, :], boxes.shape)
    slot, lane = iota(boxes.shape, 1), iota(boxes.shape, 2)
    label = jnp.sum(jnp.where((slot == lane) & (slot < 6), labels, 0.0), axis=2, keepdims=True)
    label = label.reshape(rows, 1).astype(I32)
    lane = iota((1, 128), 1)
    k = iota((1, 512), 1)
    group = 2 * (k >> 6) - 1 + ((k >> 4) & 3)
    wanted = ((k & 1) * 8 + ((k >> 1) & 7)) * 16 + group + 1
    wanted = jnp.where((group >= 0) & (group < 16), wanted, -1)
    pick = ones_where(label == wanted)
    got = lax.dot_general(pick, inbox, (((0,), (0,)), ((), ())), preferred_element_type=F32)
    for target in range(8):
        rows = got[64 * target : 64 * target + 64]
        halo = jnp.where(lane < 64, rows[48:64], rows[0:16])
        out_ref[48 * target : 48 * target + 48] = jnp.concatenate([rows[16:48], halo], axis=0).astype(BF16)


def dot_nt(x, w):
    return lax.dot_general(x, w, (((1,), (1,)), ((), ())), preferred_element_type=F32)


def silu(v):
    half = 0.5 * v
    return half * jnp.tanh(half) + half


def decode_kernel(
    recv_ref, w1_ref, wc_hbm, w0_hbm, wp_hbm, vec_ref, out_hbm,
    grid_ref, x_ref, a_ref, u_ref, r_ref, fin_ref, wc_ref, w0_ref, wp_ref, out_ref, sems, out_sems,
):
    s = lax.axis_index("seq")
    t = lax.axis_index("tile")
    wc_copy = pltpu.make_async_copy(wc_hbm, wc_ref, sems.at[0])
    w0_copy = pltpu.make_async_copy(w0_hbm, w0_ref, sems.at[1])
    wp_copy = pltpu.make_async_copy(wp_hbm, wp_ref.at[pl.ds(64, 192)], sems.at[2])
    wc_copy.start()
    w0_copy.start()
    wp_copy.start()
    b1, g1, bc, g2, b3 = (vec_ref[n : n + 1, :] for n in range(5))
    lane = iota((1, 128), 1)

    i, k = iota((384, 128), 0), iota((1, 384), 1)
    source = k // 48
    key_i = (i >> 4) * 32 + 2 * (i & 7) + ((i >> 3) & 1)
    key_k = ((k - 48 * source) >> 1) * 32 + 2 * source + (k & 1)
    pick = [ones_where(key_i == key_k[:, 128 * n : 128 * n + 128]) for n in range(3)]
    grid_ref[...] = jnp.dot(
        jnp.concatenate(pick, axis=1), recv_ref[...], preferred_element_type=F32
    ).reshape(3, 8, 16, 128)

    def windows(y):
        later = iota((8, 128), 0) > 0
        tiles = [[], [], []]
        for c in (2, 0, 1):
            now = grid_ref[c, y]
            even, odd = now[0:8], now[8:16]
            even_before = jnp.where(later, pltpu.roll(even, 1, 0), 0.0)
            odd_before = jnp.where(later, pltpu.roll(odd, 1, 0), 0.0)
            tiles[0].append(jnp.concatenate([even_before, odd_before], axis=0))
            tiles[1].append(jnp.concatenate([odd_before, even], axis=0))
            tiles[2].append(now)
        for group in tiles:
            group.append(group[0])
        for ix in range(18):
            c, o = divmod((ix + 6) * 16, 128)

            def window(d, to):
                tile = tiles[d][c]
                if o + 48 > 128:
                    tile = jnp.where(lane >= o, tile, tiles[d][c + 1])
                shift = (to - o) % 128
                return pltpu.roll(tile, shift, 1) if shift else tile

            x_ref[y, ix, :, 0:128] = jnp.where(lane < 64, window(0, 0), window(1, 64)).astype(BF16)
            x_ref[y, ix, :, 128:256] = window(2, 0).astype(BF16)

    for y in range(8):
        windows(y)

    def inside(condition):
        return jnp.where(condition, 1.0, 0.0)

    has_low_row, has_high_row = inside(t > 0), inside(t < lax.axis_size("tile") - 1)
    has_low_col, has_high_col = inside(s > 0), inside(s < lax.axis_size("seq") - 1)

    def first(iy):
        lhs = jnp.concatenate([x_ref[iy + d].reshape(288, 256) for d in range(3)], axis=1)
        v = jnp.dot(lhs, w1_ref[...], preferred_element_type=F32) + b1
        scale = lax.rsqrt(jnp.mean(v * v, axis=1, keepdims=True) + 1e-06)
        row = iota((288, 1), 0)
        scale = jnp.where(row < 16, scale * has_low_col, scale)
        scale = jnp.where(row >= 272, scale * has_high_col, scale)
        if iy == 0:
            scale = scale * has_low_row
        if iy == 5:
            scale = scale * has_high_row
        a_ref[iy] = silu(v * scale * g1).astype(BF16).reshape(18, 16, 384)

    for iy in range(6):
        first(iy)

    wc_copy.wait()

    def corners(ci):
        lhs = jnp.concatenate(
            [a_ref[ci + d, e : e + 17].reshape(272, 384) for d in range(2) for e in range(2)],
            axis=1,
        )
        acc = dot_nt(lhs, wc_ref[...])
        for d in range(2):
            u = (acc[:, 384 * d : 384 * d + 384] + bc).astype(BF16)
            u_ref[2 * ci + d] = u.reshape(17, 16, 384)
            u = u.astype(F32)
            sq = u * u
            mid = sq[:, 128:256]
            low = jnp.sum(sq[:, 0:128] + jnp.where(lane < 64, mid, 0.0), axis=1, keepdims=True)
            top = jnp.sum(sq[:, 256:384] + jnp.where(lane < 64, 0.0, mid), axis=1, keepdims=True)
            low = lax.rsqrt(low * (1 / 192) + 1e-06)
            top = lax.rsqrt(top * (1 / 192) + 1e-06)
            row = iota((272, 1), 0)
            low = jnp.where(row >= 256, low * has_high_col, low)
            top = jnp.where(row < 16, top * has_low_col, top)
            if 2 * ci + d == 0:
                low, top = low * has_low_row, top * has_low_row
            if 2 * ci + d == 9:
                low, top = low * has_high_row, top * has_high_row
            low = jnp.broadcast_to(low, (272, 128))
            top = jnp.broadcast_to(top, (272, 128))
            scale = jnp.concatenate([low, jnp.where(lane < 64, low, top), top], axis=1)
            r = silu(u * scale * g2).reshape(17, 16, 384)
            d2, d3 = r[:, 0:8], r[:, 8:16]
            later = iota((1, 8, 384), 1) > 0
            d0 = jnp.where(later, pltpu.roll(d2, 1, 1), 0.0)
            d1 = jnp.where(later, pltpu.roll(d3, 1, 1), 0.0)
            for n, v in enumerate((d0 - d2, d1 + d2, d2 - d1, d1 - d3)):
                r_ref[n, 0, 2 * ci + d] = v[0:16].reshape(8, 16, 384).astype(BF16)
                r_ref[n, 1, 2 * ci + d] = v[1:17].reshape(8, 16, 384).astype(BF16)

    for ci in range(5):
        corners(ci)

    def residual(i, carry):
        even, odd = [], []
        for n in range(4):
            def tap(shift, e, low, high):
                return jnp.concatenate(
                    [
                        r_ref[n, shift, pl.ds(e, 8), i * NI + k, :, low:high].reshape(128, high - low)
                        for k in range(NI)
                    ],
                    axis=0,
                )

            def swapped(x):
                return pltpu.roll(x.astype(F32), 64, 1)

            mids = [[tap(shift, e, 128, 256) for e in range(3)] for shift in range(2)]
            left_mid = jnp.where(lane < 64, mids[0][0].astype(F32), swapped(mids[0][1])).astype(BF16)
            right_mid = jnp.where(lane < 64, swapped(mids[1][1]), mids[1][0].astype(F32)).astype(BF16)
            rights = [tap(1, e, 256, 384) for e in range(3)] + [right_mid, mids[1][2]]
            lefts = [tap(0, e, 0, 128) for e in range(3)] + [left_mid, mids[0][2]]
            at = slice(n * 1792, n * 1792 + 1792)
            even_lhs = jnp.concatenate([tap(0, e, 0, 384) for e in range(3)] + rights, axis=1)
            odd_lhs = jnp.concatenate([tap(1, e, 0, 384) for e in range(3)] + lefts, axis=1)
            even.append(dot_nt(even_lhs, w0_ref[:, at]))
            odd.append(dot_nt(odd_lhs, wp_ref[:, at]))
        for parity in range(2):
            if parity == 0:
                p, q = (v[0] + (v[1] + v[2]) for v in (even, odd))
            else:
                p, q = (v[1] - v[2] - v[3] for v in (even, odd))
            p = p.reshape(NI, 8, 2, 8, 192)
            q = q.reshape(NI, 8, 2, 8, 256)
            for k in range(NI):
                for c in range(2):
                    m = (i * NI + k) * 2 + c
                    pk, qk = p[k, :, c], q[k, :, c]
                    now = slice(8 * parity, 8 * parity + 8)
                    left = u_ref[pl.ds(1, 8), m].astype(F32)[:, now]
                    right = u_ref[pl.ds(1, 8), m + 1].astype(F32)[:, now]
                    mid = jnp.where(lane < 64, left[..., 128:256], right[..., 128:256])
                    edge = jnp.concatenate([pk[..., 128:192], jnp.zeros((8, 8, 64), F32)], axis=2)
                    parts = (
                        pk[..., 0:128] + b3[:, 0:128] + left[..., 0:128],
                        edge + qk[..., 0:128] + b3[:, 128:256] + mid,
                        qk[..., 128:256] + b3[:, 256:384] + right[..., 256:384],
                    )
                    for z, part in enumerate(parts):
                        fin_ref[m, parity, z] = part.reshape(64, 128)
        return carry

    wp_ref[0:64, :] = jnp.zeros((64, 7168), BF16)
    w0_copy.wait()
    wp_copy.wait()
    for i in range(8 // NI):
        residual(i, 0)
    outs = []
    for f in range(16):
        for m in range(16):
            for c in range(3):
                rows = fin_ref[m, f & 1, c, pl.ds(f >> 1, 8, stride=8), :]
                out_ref[f, :, 384 * m + 128 * c : 384 * m + 128 * c + 128] = rows.astype(BF16)
        outs.append(pltpu.make_async_copy(out_ref.at[f], out_hbm.at[f], out_sems.at[f]))
        outs[-1].start()
    for copy in outs:
        copy.wait()


def prepare_kernel(
    win_hbm, wup_hbm, wres_hbm, bin_hbm, gin_hbm, bup_hbm, gres_hbm, bres_hbm,
    w1_ref, wc_hbm, w0_hbm, wp_hbm, vec_ref,
    win_ref, wup_ref, wres_ref, bin_ref, gin_ref, bup_ref, gres_ref, bres_ref,
    wc_ref, w0_ref, wp_ref, sems, in_sems, out_sems,
):
    chunks = [pl.ds(48 * n, 48) for n in range(4)]
    res_in = [
        pltpu.make_async_copy(wres_hbm.at[at], wres_ref.at[at], in_sems.at[0, n])
        for n, at in enumerate(chunks)
    ]
    up_in = [
        pltpu.make_async_copy(wup_hbm.at[at], wup_ref.at[at], in_sems.at[1, n])
        for n, at in enumerate(chunks)
    ]
    pairs = (
        (win_hbm, win_ref), (bin_hbm, bin_ref), (gin_hbm, gin_ref), (bup_hbm, bup_ref),
        (gres_hbm, gres_ref), (bres_hbm, bres_ref),
    )
    rest = [pltpu.make_async_copy(x, y, sems.at[n]) for n, (x, y) in enumerate(pairs)]
    for copy in res_in + up_in + rest:
        copy.start()

    outs = []
    zero = jnp.zeros((48, 64), BF16)
    for chunk, rows in enumerate(chunks):
        res_in[chunk].wait()
        kinds = [[], [], [], []]
        for row in range(3):
            g = [wres_ref[rows, (time * 3 + row) * 576 : (time * 3 + row) * 576 + 576] for time in range(3)]
            ends = (g[0].astype(F32) + g[2].astype(F32)) * 0.5
            mid = g[1].astype(F32) * 0.5
            for kind, tap in zip(kinds, (g[0], (ends + mid).astype(BF16), (ends - mid).astype(BF16), g[2])):
                kind.append([tap[:, e * 192 : e * 192 + 192] for e in range(3)])
        for n, w in enumerate(kinds):
            at = slice(n * 1792, n * 1792 + 1792)
            even = [w[e][x] for e in range(3) for x in (1, 0)]
            even += [w[e][2][:, 64:192] for e in range(3)]
            even += [w[1][2][:, 0:64], w[0][2][:, 0:64], zero, w[2][2][:, 0:64]]
            odd = [w[e][x] for e in range(3) for x in (2, 1)]
            odd += [w[e][0][:, 0:128] for e in range(3)]
            odd += [w[0][0][:, 128:192], w[1][0][:, 128:192], w[2][0][:, 128:192], zero]
            w0_ref[rows, at] = jnp.concatenate(even, axis=1)
            wp_ref[rows, at] = jnp.concatenate(odd, axis=1)
        outs.append(pltpu.make_async_copy(w0_ref.at[rows], w0_hbm.at[rows], out_sems.at[0, chunk]))
        outs.append(pltpu.make_async_copy(wp_ref.at[rows], wp_hbm.at[rows], out_sems.at[1, chunk]))
        outs[-2].start()
        outs[-1].start()

    taps = [[[0, 1], [2]], [[0], [1, 2]]]
    for copy in up_in:
        copy.wait()
    for dy in range(2):
        for place, dx in enumerate((1, 0)):
            to = (dy * 2 + place) * 192
            for r in range(2):
                for c in range(2):
                    total = None
                    for b in taps[dy][r]:
                        for e in taps[dx][c]:
                            at = (b * 3 + e) * 384
                            term = wup_ref[:, at : at + 384].astype(F32)
                            total = term if total is None else total + term
                    at = (r * 2 + c) * 384
                    wc_ref[to : to + 192, at : at + 384] = total.astype(BF16)
            rows = pl.ds(to, 192)
            outs.append(pltpu.make_async_copy(wc_ref.at[rows], wc_hbm.at[rows], out_sems.at[2, dy * 2 + place]))
            outs[-1].start()

    for copy in rest:
        copy.wait()
    for row in range(3):
        for time in range(3):
            at = row * 256 + time * 64
            w1_ref[at : at + 48] = win_ref[(time * 3 + row) * 48 : (time * 3 + row) * 48 + 48]
            w1_ref[at + 48 : at + 64] = jnp.zeros((16, 384), BF16)
        w1_ref[row * 256 + 192 : row * 256 + 256] = jnp.zeros((64, 384), BF16)

    vec_ref[...] = jnp.zeros((8, 384), F32)
    for row, ref in enumerate((bin_ref, gin_ref)):
        vec_ref[row : row + 1, :] = ref[...].reshape(1, 384)
    for row, ref in enumerate((bup_ref, gres_ref, bres_ref)):
        v = ref[...].reshape(1, 192)
        vec_ref[row + 2 : row + 3, :] = jnp.concatenate([v, v], axis=1)
    for copy in outs:
        copy.wait()


VMEM_SPEC = pl.BlockSpec(memory_space=pltpu.VMEM)
ANY_SPEC = pl.BlockSpec(memory_space=pl.ANY)
HBM_SPEC = pl.BlockSpec(memory_space=pltpu.HBM)


def local(latents, grid_slot, w_in, b_in, gain_in, w_up, b_up, gain_res, w_res, b_res):
    outbox = pl.pallas_call(
        outbox_kernel,
        out_shape=jax.ShapeDtypeStruct((1024, 128), BF16),
        in_specs=[VMEM_SPEC] * 2,
        out_specs=VMEM_SPEC,
        name="outbox",
    )(grid_slot.reshape(1, 128), latents)
    inbox = lax.all_to_all(
        outbox.reshape(128, 8, 128), ("seq", "tile"), split_axis=0, concat_axis=0, tiled=True
    )
    prepared = pl.pallas_call(
        prepare_kernel,
        out_shape=[
            jax.ShapeDtypeStruct((768, 384), BF16),
            pltpu.HBM((768, 1536), BF16),
            pltpu.HBM((192, 7168), BF16),
            pltpu.HBM((192, 7168), BF16),
            jax.ShapeDtypeStruct((8, 384), F32),
        ],
        in_specs=[HBM_SPEC] * 8,
        out_specs=[VMEM_SPEC] + [HBM_SPEC] * 3 + [VMEM_SPEC],
        scratch_shapes=[
            pltpu.VMEM((432, 384), BF16),
            pltpu.VMEM((192, 3456), BF16),
            pltpu.VMEM((192, 5184), BF16),
            pltpu.VMEM((384,), F32),
            pltpu.VMEM((384,), F32),
            pltpu.VMEM((192,), F32),
            pltpu.VMEM((192,), F32),
            pltpu.VMEM((192,), F32),
            pltpu.VMEM((768, 1536), BF16),
            pltpu.VMEM((192, 7168), BF16),
            pltpu.VMEM((192, 7168), BF16),
            pltpu.SemaphoreType.DMA((6,)),
            pltpu.SemaphoreType.DMA((2, 4)),
            pltpu.SemaphoreType.DMA((3, 4)),
        ],
        cost_estimate=pl.CostEstimate(flops=10_000_000, bytes_accessed=16_000_000, transcendentals=0),
        compiler_params=pltpu.CompilerParams(vmem_limit_bytes=28 * 1024 * 1024),
        name="prepare",
    )(
        *(
            pltpu.with_memory_space_constraint(w, pltpu.HBM)
            for w in (w_in, w_up.T, w_res.T, b_in, gain_in, b_up, gain_res, b_res)
        )
    )
    routed = pl.pallas_call(
        route_kernel,
        out_shape=jax.ShapeDtypeStruct((384, 128), BF16),
        in_specs=[VMEM_SPEC, ANY_SPEC],
        out_specs=VMEM_SPEC,
        compiler_params=pltpu.CompilerParams(vmem_limit_bytes=12 * 1024 * 1024),
        name="route",
    )(inbox.reshape(1024, 128), prepared[4])
    recv = lax.all_to_all(
        routed.reshape(8, 48, 128), "seq", split_axis=0, concat_axis=0, tiled=True
    ).reshape(384, 128)
    return decode(recv, *prepared)


def decode(recv, w1, wc, w0, wp, vec):
    return pl.pallas_call(
        decode_kernel,
        out_shape=jax.ShapeDtypeStruct((16, 8, 6144), BF16),
        in_specs=[VMEM_SPEC] * 2 + [HBM_SPEC] * 3 + [VMEM_SPEC],
        out_specs=HBM_SPEC,
        scratch_shapes=[
            pltpu.VMEM((3, 8, 16, 128), F32),
            pltpu.VMEM((8, 18, 16, 256), BF16),
            pltpu.VMEM((6, 18, 16, 384), BF16),
            pltpu.VMEM((10, 17, 16, 384), BF16),
            pltpu.VMEM((4, 2, 10, 8, 16, 384), BF16),
            pltpu.VMEM((16, 2, 3, 64, 128), F32),
            pltpu.VMEM((768, 1536), BF16),
            pltpu.VMEM((192, 7168), BF16),
            pltpu.VMEM((256, 7168), BF16),
            pltpu.VMEM((16, 8, 6144), BF16),
            pltpu.SemaphoreType.DMA((3,)),
            pltpu.SemaphoreType.DMA((16,)),
        ],
        compiler_params=pltpu.CompilerParams(vmem_limit_bytes=44 * 1024 * 1024),
        name="decode",
    )(recv, w1, *(pltpu.with_memory_space_constraint(w, pltpu.HBM) for w in (wc, w0, wp)), vec)


def solution(mesh):
    return jax.shard_map(
        local,
        mesh=mesh,
        in_specs=(P(("seq", "tile"), None), P(("seq", "tile"))) + (P(),) * 8,
        out_specs=P(None, "tile", "seq"),
        check_vma=False,
    )
```

```python
import jax
import jax.numpy as jnp
from jax import lax
from jax.experimental import pallas as pl
from jax.experimental.pallas import tpu as pltpu
from jax.sharding import PartitionSpec as P

F32 = jnp.float32
BF16 = jnp.bfloat16
I32 = jnp.int32
NI = 8


def iota(shape, dim):
    return lax.broadcasted_iota(I32, shape, dim)


def ones_where(cond):
    return jnp.where(cond, 1.0, 0.0).astype(BF16)


def outbox_kernel(slot_ref, lat_hbm, out_hbm, lat_ref, out_ref, sem, out_sems):
    fetch = pltpu.make_async_copy(lat_hbm, lat_ref, sem)
    fetch.start()
    n = 128
    row = jnp.broadcast_to(slot_ref[...], (n, n))
    col = jnp.transpose(row)
    i, j = iota((n, n), 0), iota((n, n), 1)
    same = (row >> 7) == (col >> 7)
    rank_row = jnp.sum(jnp.where(same & (i < j), 1, 0), axis=0, keepdims=True)
    rank_col = jnp.sum(jnp.where(same & (j < i), 1, 0), axis=1, keepdims=True)

    def keys(slot, rank):
        target = slot >> 7
        band = target & 15
        frame, high, group = (slot >> 6) & 1, (slot >> 4) & 3, slot & 15
        upper = high < 2
        halo_target = jnp.where(upper, target - 1, target + 1)
        inside = (upper & (band > 0)) | ((high >= 2) & (band < 15))
        halo_target = jnp.where(inside, halo_target, -1000)
        halo_slot = jnp.where(upper, 4, 2) + rank
        own_label = (frame * 8 + high + 2) * 16 + group + 1
        halo_label = (frame * 8 + jnp.where(upper, high + 6, high - 2)) * 16 + group + 1
        return target, halo_target, halo_slot, own_label, halo_label

    target, halo_target, halo_slot, _, _ = keys(slot_ref[...], rank_row)
    _, _, halo_slot_col, own_label, halo_label = keys(col, rank_col)
    own_table = jnp.where(j == rank_col, own_label, 0).astype(F32).astype(BF16)
    halo_table = jnp.where(j == halo_slot_col, halo_label, 0).astype(F32).astype(BF16)

    fetch.wait()
    outs = []
    for chunk in range(4):
        rows = pl.ds(2 * n * chunk, 2 * n)
        q = iota((2 * n, n), 0) + 2 * n * chunk
        pick = ones_where((q == target * 8 + rank_row) | (q == halo_target * 8 + halo_slot))
        pick_own = ones_where(q == target * 8 + 6)
        pick_halo = ones_where(q == halo_target * 8 + 6)
        out = jnp.dot(pick, lat_ref[...], preferred_element_type=F32)
        out += jnp.dot(pick_own, own_table, preferred_element_type=F32)
        out += jnp.dot(pick_halo, halo_table, preferred_element_type=F32)
        out_ref[rows, :] = out.astype(BF16)
        outs.append(pltpu.make_async_copy(out_ref.at[rows], out_hbm.at[rows], out_sems.at[chunk]))
        outs[-1].start()
    for copy in outs:
        copy.wait()


def route_kernel(inbox_ref, after_ref, out_ref):
    rows = inbox_ref.shape[0]
    inbox = inbox_ref[...]
    boxes = inbox.astype(F32).reshape(rows // 8, 8, 128)
    labels = jnp.broadcast_to(boxes[:, 6:7, :], boxes.shape)
    slot, lane = iota(boxes.shape, 1), iota(boxes.shape, 2)
    label = jnp.sum(jnp.where((slot == lane) & (slot < 6), labels, 0.0), axis=2, keepdims=True)
    label = label.reshape(rows, 1).astype(I32)
    lane = iota((1, 128), 1)
    k = iota((1, 512), 1)
    group = 2 * (k >> 6) - 1 + ((k >> 4) & 3)
    wanted = ((k & 1) * 8 + ((k >> 1) & 7)) * 16 + group + 1
    wanted = jnp.where((group >= 0) & (group < 16), wanted, -1)
    pick = ones_where(label == wanted)
    got = lax.dot_general(pick, inbox, (((0,), (0,)), ((), ())), preferred_element_type=F32)
    for target in range(8):
        rows = got[64 * target : 64 * target + 64]
        halo = jnp.where(lane < 64, rows[48:64], rows[0:16])
        out_ref[48 * target : 48 * target + 48] = jnp.concatenate([rows[16:48], halo], axis=0).astype(BF16)


def dot_nt(x, w):
    return lax.dot_general(x, w, (((1,), (1,)), ((), ())), preferred_element_type=F32)


def silu(v):
    half = 0.5 * v
    return half * jnp.tanh(half) + half


def decode_kernel(
    recv_ref, w1_ref, wc_hbm, w0_hbm, wp_hbm, vec_ref, out_hbm,
    grid_ref, x_ref, a_ref, u_ref, r_ref, fin_ref, wc_ref, w0_ref, wp_ref, out_ref, sems, out_sems,
):
    s = lax.axis_index("seq")
    t = lax.axis_index("tile")
    wc_copy = pltpu.make_async_copy(wc_hbm, wc_ref, sems.at[0])
    w0_copy = pltpu.make_async_copy(w0_hbm, w0_ref, sems.at[1])
    wp_copy = pltpu.make_async_copy(wp_hbm, wp_ref.at[pl.ds(64, 192)], sems.at[2])
    wc_copy.start()
    w0_copy.start()
    wp_copy.start()
    b1, g1, bc, g2, b3 = (vec_ref[n : n + 1, :] for n in range(5))
    lane = iota((1, 128), 1)

    i, k = iota((384, 128), 0), iota((1, 384), 1)
    source = k // 48
    key_i = (i >> 4) * 32 + 2 * (i & 7) + ((i >> 3) & 1)
    key_k = ((k - 48 * source) >> 1) * 32 + 2 * source + (k & 1)
    pick = [ones_where(key_i == key_k[:, 128 * n : 128 * n + 128]) for n in range(3)]
    grid_ref[...] = jnp.dot(
        jnp.concatenate(pick, axis=1), recv_ref[...], preferred_element_type=F32
    ).reshape(3, 8, 16, 128)

    def windows(y):
        later = iota((8, 128), 0) > 0
        tiles = [[], [], []]
        for c in (2, 0, 1):
            now = grid_ref[c, y]
            even, odd = now[0:8], now[8:16]
            even_before = jnp.where(later, pltpu.roll(even, 1, 0), 0.0)
            odd_before = jnp.where(later, pltpu.roll(odd, 1, 0), 0.0)
            tiles[0].append(jnp.concatenate([even_before, odd_before], axis=0))
            tiles[1].append(jnp.concatenate([odd_before, even], axis=0))
            tiles[2].append(now)
        for group in tiles:
            group.append(group[0])
        for ix in range(18):
            c, o = divmod((ix + 6) * 16, 128)

            def window(d, to):
                tile = tiles[d][c]
                if o + 48 > 128:
                    tile = jnp.where(lane >= o, tile, tiles[d][c + 1])
                shift = (to - o) % 128
                return pltpu.roll(tile, shift, 1) if shift else tile

            x_ref[y, ix, :, 0:128] = jnp.where(lane < 64, window(0, 0), window(1, 64)).astype(BF16)
            x_ref[y, ix, :, 128:256] = window(2, 0).astype(BF16)

    for y in range(8):
        windows(y)

    def inside(condition):
        return jnp.where(condition, 1.0, 0.0)

    has_low_row, has_high_row = inside(t > 0), inside(t < lax.axis_size("tile") - 1)
    has_low_col, has_high_col = inside(s > 0), inside(s < lax.axis_size("seq") - 1)

    def first(iy):
        lhs = jnp.concatenate([x_ref[iy + d].reshape(288, 256) for d in range(3)], axis=1)
        v = jnp.dot(lhs, w1_ref[...], preferred_element_type=F32) + b1
        scale = lax.rsqrt(jnp.mean(v * v, axis=1, keepdims=True) + 1e-06)
        row = iota((288, 1), 0)
        scale = jnp.where(row < 16, scale * has_low_col, scale)
        scale = jnp.where(row >= 272, scale * has_high_col, scale)
        if iy == 0:
            scale = scale * has_low_row
        if iy == 5:
            scale = scale * has_high_row
        a_ref[iy] = silu(v * scale * g1).astype(BF16).reshape(18, 16, 384)

    for iy in range(6):
        first(iy)

    wc_copy.wait()

    def corners(ci):
        lhs = jnp.concatenate(
            [a_ref[ci + d, e : e + 17].reshape(272, 384) for d in range(2) for e in range(2)],
            axis=1,
        )
        acc = dot_nt(lhs, wc_ref[...])
        for d in range(2):
            u = (acc[:, 384 * d : 384 * d + 384] + bc).astype(BF16)
            u_ref[2 * ci + d] = u.reshape(17, 16, 384)
            u = u.astype(F32)
            sq = u * u
            mid = sq[:, 128:256]
            low = jnp.sum(sq[:, 0:128] + jnp.where(lane < 64, mid, 0.0), axis=1, keepdims=True)
            top = jnp.sum(sq[:, 256:384] + jnp.where(lane < 64, 0.0, mid), axis=1, keepdims=True)
            low = lax.rsqrt(low * (1 / 192) + 1e-06)
            top = lax.rsqrt(top * (1 / 192) + 1e-06)
            row = iota((272, 1), 0)
            low = jnp.where(row >= 256, low * has_high_col, low)
            top = jnp.where(row < 16, top * has_low_col, top)
            if 2 * ci + d == 0:
                low, top = low * has_low_row, top * has_low_row
            if 2 * ci + d == 9:
                low, top = low * has_high_row, top * has_high_row
            low = jnp.broadcast_to(low, (272, 128))
            top = jnp.broadcast_to(top, (272, 128))
            scale = jnp.concatenate([low, jnp.where(lane < 64, low, top), top], axis=1)
            r = silu(u * scale * g2).reshape(17, 16, 384)
            d2, d3 = r[:, 0:8], r[:, 8:16]
            later = iota((1, 8, 384), 1) > 0
            d0 = jnp.where(later, pltpu.roll(d2, 1, 1), 0.0)
            d1 = jnp.where(later, pltpu.roll(d3, 1, 1), 0.0)
            for n, v in enumerate((d0 - d2, d1 + d2, d2 - d1, d1 - d3)):
                r_ref[n, 0, 2 * ci + d] = v[0:16].reshape(8, 16, 384).astype(BF16)
                r_ref[n, 1, 2 * ci + d] = v[1:17].reshape(8, 16, 384).astype(BF16)

    for ci in range(5):
        corners(ci)

    def residual(i, carry):
        even, odd = [], []
        for n in range(4):
            def tap(shift, e, low, high):
                return jnp.concatenate(
                    [
                        r_ref[n, shift, pl.ds(e, 8), i * NI + k, :, low:high].reshape(128, high - low)
                        for k in range(NI)
                    ],
                    axis=0,
                )

            def swapped(x):
                return pltpu.roll(x.astype(F32), 64, 1)

            mids = [[tap(shift, e, 128, 256) for e in range(3)] for shift in range(2)]
            left_mid = jnp.where(lane < 64, mids[0][0].astype(F32), swapped(mids[0][1])).astype(BF16)
            right_mid = jnp.where(lane < 64, swapped(mids[1][1]), mids[1][0].astype(F32)).astype(BF16)
            rights = [tap(1, e, 256, 384) for e in range(3)] + [right_mid, mids[1][2]]
            lefts = [tap(0, e, 0, 128) for e in range(3)] + [left_mid, mids[0][2]]
            at = slice(n * 1792, n * 1792 + 1792)
            even_lhs = jnp.concatenate([tap(0, e, 0, 384) for e in range(3)] + rights, axis=1)
            odd_lhs = jnp.concatenate([tap(1, e, 0, 384) for e in range(3)] + lefts, axis=1)
            even.append(dot_nt(even_lhs, w0_ref[:, at]))
            odd.append(dot_nt(odd_lhs, wp_ref[:, at]))
        for parity in range(2):
            if parity == 0:
                p, q = (v[0] + (v[1] + v[2]) for v in (even, odd))
            else:
                p, q = (v[1] - v[2] - v[3] for v in (even, odd))
            p = p.reshape(NI, 8, 2, 8, 192)
            q = q.reshape(NI, 8, 2, 8, 256)
            for k in range(NI):
                for c in range(2):
                    m = (i * NI + k) * 2 + c
                    pk, qk = p[k, :, c], q[k, :, c]
                    now = slice(8 * parity, 8 * parity + 8)
                    left = u_ref[pl.ds(1, 8), m].astype(F32)[:, now]
                    right = u_ref[pl.ds(1, 8), m + 1].astype(F32)[:, now]
                    mid = jnp.where(lane < 64, left[..., 128:256], right[..., 128:256])
                    edge = jnp.concatenate([pk[..., 128:192], jnp.zeros((8, 8, 64), F32)], axis=2)
                    parts = (
                        pk[..., 0:128] + b3[:, 0:128] + left[..., 0:128],
                        edge + qk[..., 0:128] + b3[:, 128:256] + mid,
                        qk[..., 128:256] + b3[:, 256:384] + right[..., 256:384],
                    )
                    for z, part in enumerate(parts):
                        fin_ref[m, parity, z] = part.reshape(64, 128)
        return carry

    wp_ref[0:64, :] = jnp.zeros((64, 7168), BF16)
    w0_copy.wait()
    wp_copy.wait()
    for i in range(8 // NI):
        residual(i, 0)
    outs = []
    for f in range(16):
        for m in range(16):
            for c in range(3):
                rows = fin_ref[m, f & 1, c, pl.ds(f >> 1, 8, stride=8), :]
                out_ref[f, :, 384 * m + 128 * c : 384 * m + 128 * c + 128] = rows.astype(BF16)
        outs.append(pltpu.make_async_copy(out_ref.at[f], out_hbm.at[f], out_sems.at[f]))
        outs[-1].start()
    for copy in outs:
        copy.wait()


def prepare_kernel(
    win_hbm, wup_hbm, wres_hbm, bin_hbm, gin_hbm, bup_hbm, gres_hbm, bres_hbm,
    w1_ref, wc_hbm, w0_hbm, wp_hbm, vec_ref,
    win_ref, wup_ref, wres_ref, bin_ref, gin_ref, bup_ref, gres_ref, bres_ref,
    wc_ref, w0_ref, wp_ref, sems, in_sems, out_sems,
):
    chunks = [pl.ds(48 * n, 48) for n in range(4)]
    res_in = [
        pltpu.make_async_copy(wres_hbm.at[at], wres_ref.at[at], in_sems.at[0, n])
        for n, at in enumerate(chunks)
    ]
    up_in = [
        pltpu.make_async_copy(wup_hbm.at[at], wup_ref.at[at], in_sems.at[1, n])
        for n, at in enumerate(chunks)
    ]
    pairs = (
        (win_hbm, win_ref), (bin_hbm, bin_ref), (gin_hbm, gin_ref), (bup_hbm, bup_ref),
        (gres_hbm, gres_ref), (bres_hbm, bres_ref),
    )
    rest = [pltpu.make_async_copy(x, y, sems.at[n]) for n, (x, y) in enumerate(pairs)]
    for copy in res_in + up_in + rest:
        copy.start()

    outs = []
    zero = jnp.zeros((48, 64), BF16)
    for chunk, rows in enumerate(chunks):
        res_in[chunk].wait()
        kinds = [[], [], [], []]
        for row in range(3):
            g = [wres_ref[rows, (time * 3 + row) * 576 : (time * 3 + row) * 576 + 576] for time in range(3)]
            ends = (g[0].astype(F32) + g[2].astype(F32)) * 0.5
            mid = g[1].astype(F32) * 0.5
            for kind, tap in zip(kinds, (g[0], (ends + mid).astype(BF16), (ends - mid).astype(BF16), g[2])):
                kind.append([tap[:, e * 192 : e * 192 + 192] for e in range(3)])
        for n, w in enumerate(kinds):
            at = slice(n * 1792, n * 1792 + 1792)
            even = [w[e][x] for e in range(3) for x in (1, 0)]
            even += [w[e][2][:, 64:192] for e in range(3)]
            even += [w[1][2][:, 0:64], w[0][2][:, 0:64], zero, w[2][2][:, 0:64]]
            odd = [w[e][x] for e in range(3) for x in (2, 1)]
            odd += [w[e][0][:, 0:128] for e in range(3)]
            odd += [w[0][0][:, 128:192], w[1][0][:, 128:192], w[2][0][:, 128:192], zero]
            w0_ref[rows, at] = jnp.concatenate(even, axis=1)
            wp_ref[rows, at] = jnp.concatenate(odd, axis=1)
        outs.append(pltpu.make_async_copy(w0_ref.at[rows], w0_hbm.at[rows], out_sems.at[0, chunk]))
        outs.append(pltpu.make_async_copy(wp_ref.at[rows], wp_hbm.at[rows], out_sems.at[1, chunk]))
        outs[-2].start()
        outs[-1].start()

    taps = [[[0, 1], [2]], [[0], [1, 2]]]
    for copy in up_in:
        copy.wait()
    for dy in range(2):
        for place, dx in enumerate((1, 0)):
            to = (dy * 2 + place) * 192
            for r in range(2):
                for c in range(2):
                    total = None
                    for b in taps[dy][r]:
                        for e in taps[dx][c]:
                            at = (b * 3 + e) * 384
                            term = wup_ref[:, at : at + 384].astype(F32)
                            total = term if total is None else total + term
                    at = (r * 2 + c) * 384
                    wc_ref[to : to + 192, at : at + 384] = total.astype(BF16)
            rows = pl.ds(to, 192)
            outs.append(pltpu.make_async_copy(wc_ref.at[rows], wc_hbm.at[rows], out_sems.at[2, dy * 2 + place]))
            outs[-1].start()

    for copy in rest:
        copy.wait()
    for row in range(3):
        for time in range(3):
            at = row * 256 + time * 64
            w1_ref[at : at + 48] = win_ref[(time * 3 + row) * 48 : (time * 3 + row) * 48 + 48]
            w1_ref[at + 48 : at + 64] = jnp.zeros((16, 384), BF16)
        w1_ref[row * 256 + 192 : row * 256 + 256] = jnp.zeros((64, 384), BF16)

    vec_ref[...] = jnp.zeros((8, 384), F32)
    for row, ref in enumerate((bin_ref, gin_ref)):
        vec_ref[row : row + 1, :] = ref[...].reshape(1, 384)
    for row, ref in enumerate((bup_ref, gres_ref, bres_ref)):
        v = ref[...].reshape(1, 192)
        vec_ref[row + 2 : row + 3, :] = jnp.concatenate([v, v], axis=1)
    for copy in outs:
        copy.wait()


VMEM_SPEC = pl.BlockSpec(memory_space=pltpu.VMEM)
ANY_SPEC = pl.BlockSpec(memory_space=pl.ANY)
HBM_SPEC = pl.BlockSpec(memory_space=pltpu.HBM)


def local(latents, grid_slot, w_in, b_in, gain_in, w_up, b_up, gain_res, w_res, b_res):
    outbox = pl.pallas_call(
        outbox_kernel,
        out_shape=pltpu.HBM((1024, 128), BF16),
        in_specs=[VMEM_SPEC, HBM_SPEC],
        out_specs=HBM_SPEC,
        scratch_shapes=[
            pltpu.VMEM((128, 128), BF16),
            pltpu.VMEM((1024, 128), BF16),
            pltpu.SemaphoreType.DMA,
            pltpu.SemaphoreType.DMA((4,)),
        ],
        name="outbox",
    )(grid_slot.reshape(1, 128), pltpu.with_memory_space_constraint(latents, pltpu.HBM))
    inbox = lax.all_to_all(
        outbox.reshape(128, 8, 128), ("seq", "tile"), split_axis=0, concat_axis=0, tiled=True
    )
    prepared = pl.pallas_call(
        prepare_kernel,
        out_shape=[
            jax.ShapeDtypeStruct((768, 384), BF16),
            pltpu.HBM((768, 1536), BF16),
            pltpu.HBM((192, 7168), BF16),
            pltpu.HBM((192, 7168), BF16),
            jax.ShapeDtypeStruct((8, 384), F32),
        ],
        in_specs=[HBM_SPEC] * 8,
        out_specs=[VMEM_SPEC] + [HBM_SPEC] * 3 + [VMEM_SPEC],
        scratch_shapes=[
            pltpu.VMEM((432, 384), BF16),
            pltpu.VMEM((192, 3456), BF16),
            pltpu.VMEM((192, 5184), BF16),
            pltpu.VMEM((384,), F32),
            pltpu.VMEM((384,), F32),
            pltpu.VMEM((192,), F32),
            pltpu.VMEM((192,), F32),
            pltpu.VMEM((192,), F32),
            pltpu.VMEM((768, 1536), BF16),
            pltpu.VMEM((192, 7168), BF16),
            pltpu.VMEM((192, 7168), BF16),
            pltpu.SemaphoreType.DMA((6,)),
            pltpu.SemaphoreType.DMA((2, 4)),
            pltpu.SemaphoreType.DMA((3, 4)),
        ],
        cost_estimate=pl.CostEstimate(flops=10_000_000, bytes_accessed=16_000_000, transcendentals=0),
        compiler_params=pltpu.CompilerParams(vmem_limit_bytes=28 * 1024 * 1024),
        name="prepare",
    )(
        *(
            pltpu.with_memory_space_constraint(w, pltpu.HBM)
            for w in (w_in, w_up.T, w_res.T, b_in, gain_in, b_up, gain_res, b_res)
        )
    )
    routed = pl.pallas_call(
        route_kernel,
        out_shape=jax.ShapeDtypeStruct((384, 128), BF16),
        in_specs=[VMEM_SPEC, ANY_SPEC],
        out_specs=VMEM_SPEC,
        compiler_params=pltpu.CompilerParams(vmem_limit_bytes=12 * 1024 * 1024),
        name="route",
    )(inbox.reshape(1024, 128), prepared[4])
    recv = lax.all_to_all(
        routed.reshape(8, 48, 128), "seq", split_axis=0, concat_axis=0, tiled=True
    ).reshape(384, 128)
    return decode(recv, *prepared)


def decode(recv, w1, wc, w0, wp, vec):
    return pl.pallas_call(
        decode_kernel,
        out_shape=jax.ShapeDtypeStruct((16, 8, 6144), BF16),
        in_specs=[VMEM_SPEC] * 2 + [HBM_SPEC] * 3 + [VMEM_SPEC],
        out_specs=HBM_SPEC,
        scratch_shapes=[
            pltpu.VMEM((3, 8, 16, 128), F32),
            pltpu.VMEM((8, 18, 16, 256), BF16),
            pltpu.VMEM((6, 18, 16, 384), BF16),
            pltpu.VMEM((10, 17, 16, 384), BF16),
            pltpu.VMEM((4, 2, 10, 8, 16, 384), BF16),
            pltpu.VMEM((16, 2, 3, 64, 128), F32),
            pltpu.VMEM((768, 1536), BF16),
            pltpu.VMEM((192, 7168), BF16),
            pltpu.VMEM((256, 7168), BF16),
            pltpu.VMEM((16, 8, 6144), BF16),
            pltpu.SemaphoreType.DMA((3,)),
            pltpu.SemaphoreType.DMA((16,)),
        ],
        compiler_params=pltpu.CompilerParams(vmem_limit_bytes=44 * 1024 * 1024),
        name="decode",
    )(recv, w1, *(pltpu.with_memory_space_constraint(w, pltpu.HBM) for w in (wc, w0, wp)), vec)


def solution(mesh):
    return jax.shard_map(
        local,
        mesh=mesh,
        in_specs=(P(("seq", "tile"), None), P(("seq", "tile"))) + (P(),) * 8,
        out_specs=P(None, "tile", "seq"),
        check_vma=False,
    )
```
